256 devices in a mesh: ctx: 4 (over x_hi, core), exp: 64 (over x_lo, z, y).
Axes of the slice: x: 4 (x_hi: 2, x_lo: 2; x = x_hi * 2 + x_lo), y: 4, z: 8, core: 2. Of those that a mesh axis runs over, the one named last changes fastest.
Arguments:
- tokens: bfloat16 [64, 512, 1024], P('exp', 'ctx'), may hold values from -300 to 300, as said below
- expert_ids: int32 [64, 512, 2], P('exp', 'ctx'), may hold values from 0 to 63, all different within a row; in each aligned block of 128 rows (0 to 127, 128 to 255, ..., all dimensions but the last counted through in order) at most 6 rows name the same one
- attn_gain: float32 [1024], replicated, may hold values from 0.1 to 1.9
- w_query: bfloat16 [1024, 1024], P('exp'), may hold values from -0.1875 to 0.1875
- w_kv: bfloat16 [1024, 256], P('exp'), may hold values from -0.1875 to 0.1875
- w_out: bfloat16 [1024, 1024], P('exp'), may hold values from -0.1875 to 0.1875
- moe_gain: float32 [1024], replicated, may hold values from 0.1 to 1.9
- router: bfloat16 [1024, 64], replicated, may hold values from -0.375 to 0.375
- w_gate: bfloat16 [64, 1024, 4096], P('exp', None, 'ctx'), may hold values from -0.1875 to 0.1875
- w_up: bfloat16 [64, 1024, 4096], P('exp', None, 'ctx'), may hold values from -0.1875 to 0.1875
- w_down: bfloat16 [64, 4096, 1024], P('exp', 'ctx'), may hold values from -0.1875 to 0.1875
Outputs:
- attention_out: bfloat16 [64, 512, 1024], P('exp', 'ctx')
- expert_mix: bfloat16 [64, 512, 1024], P('exp', 'ctx')
The draws below stay inside these ranges and needn't reach their ends.
Inputs may be any that keep to these rules, and one draw needn't show every extreme that they name: `expert_ids`: each row names 2 different experts. In the rows of one device (aligned blocks of 128 positions) no expert is named more than 6 times, a bound that some block reaches in every draw. `tokens`: each token and each feature carries its own scale.
All inputs are finite; a program needn't handle non-finite values.
Results may differ from the reference program's by a relative error of at most 0.018.
Values may be sent and summed in bfloat16 or wider, within the bound.
A program may use at most 128 MiB of HBM per device.

```python
import math
import jax
import jax.numpy as jnp
import numpy as np
from jax import lax

D = 1024
HEADS = 8
HD = 128
EFF = 4096
TOP = 2
TOK_DEV = 128
EXPERTS = 64
LENGTH = 512
DOMAINS = 64
CAP = 6
N_CTX = 4


def draw_tokens(key, part):
    key_base, key_rows, key_cols = jax.random.split(key, 3)
    shape = (DOMAINS, LENGTH, D)
    base = jax.random.normal(key_base, shape, jnp.float32)
    row_scale = jnp.exp(jax.random.uniform(key_rows, (DOMAINS, LENGTH, 1), jnp.float32, 0.0, math.log(10.0)))
    col_scale = jnp.exp(jax.random.uniform(key_cols, (1, 1, D), jnp.float32, -1.2, 1.2))
    return (base * row_scale * col_scale).astype(jnp.bfloat16)


def steps_of(stream_key, dims, pieces, smallest, top_value):
    loudness = 1.0
    for axis_at, parts in pieces:
        steps = jax.random.uniform(jax.random.fold_in(jax.random.fold_in(stream_key, 6), axis_at), (parts,), jnp.float32, smallest / len(pieces), top_value / len(pieces))
        loudness = loudness * jnp.repeat(jnp.exp(steps), dims[axis_at] // parts).reshape((-1,) + (1,) * (len(dims) - 1 - axis_at))
    return loudness


def shared_out(rng, own, number, rows, count, top, reach, skew):
    order = jax.random.permutation(rng, count)
    crowded, ordinary = shares(count, rows * top, reach, skew, True), shares(count, rows * top, reach, skew, False)
    places = jnp.arange(count)

    def named(sizes, offset_by):
        used = int((sizes > 0).sum())
        fixed = max(1, used // 4)
        moved = fixed + (places - fixed + offset_by * (used - fixed)) % max(1, count - fixed)
        return jnp.zeros((count,), jnp.int32).at[order[jnp.where(places < fixed, places, moved)]].set(jnp.asarray(sizes, jnp.int32))

    sizes = jnp.where(number % 4 == 0, named(crowded, number // 4), named(ordinary, number - number // 4 - 1))
    mixed = jax.random.permutation(jax.random.fold_in(own, 3), count)
    source_of, taker = mixed[0:count // 2 * 2:2], mixed[1:count // 2 * 2:2]
    margin = jnp.minimum(sizes[source_of] - 1, reach - sizes[taker]) // 2
    margin = jnp.where((source_of == order[0]) | (taker == order[0]) | (sizes[taker] == 0), 0, jnp.maximum(margin, 0))
    moved = jax.random.randint(jax.random.fold_in(own, 4), (count // 2,), 0, 1 << 20) % (margin + 1)
    sizes = sizes.at[source_of].add(-moved).at[taker].add(moved)
    labels = jnp.searchsorted(jnp.cumsum(sizes), jnp.arange(rows * top), side="right").astype(jnp.int32)
    table = labels.reshape(top, rows).T
    table = table[jax.random.permutation(jax.random.fold_in(own, 1), rows)]
    offset_by = jax.random.randint(jax.random.fold_in(own, 2), (rows, 1), 0, top)
    return jnp.take_along_axis(table, (jnp.arange(top)[None, :] + offset_by) % top, axis=1)


def shares(count, total, bound, skew, full):
    loads = [(1 << 20) // math.isqrt(grade ** skew) + 1 for grade in range(1, count + 1)]
    largest = bound if full else min(bound, max(-(-total // count), total * loads[0] // sum(loads)))
    least = 1 if total - largest >= count - 1 else 0
    given, surplus = [largest] + [least] * (count - 1), total - largest - least * (count - 1)
    while surplus > 0:
        candidates = [i for i in range(1, count) if given[i] < largest] or [i for i in range(1, count) if given[i] < bound]
        whole, remaining = sum([loads[i] for i in candidates]), surplus
        for i in candidates:
            extra = min(bound - given[i], max(1, remaining * loads[i] // whole), surplus)
            given[i] = given[i] + extra
            surplus = surplus - extra
    return np.array(given)


def centred(rng, extent, deviation, limit, cuts=(), kind=jnp.bfloat16):
    array = jax.random.normal(rng, extent, jnp.float32) * deviation
    if len(cuts) > 0:
        array = steps_of(rng, extent, cuts, -0.22, 0.18) * array
    return jnp.clip(array, min=-limit, max=limit).astype(kind)


def setup_inputs(seed: int = 0) -> dict:
    splits = jax.random.split(jax.random.key(seed), 12)
    tokens = draw_tokens(jax.random.fold_in(splits[11], 71), 0)
    expert_ids_keys = jax.random.split(jax.random.fold_in(splits[1], 1), DOMAINS * LENGTH // TOK_DEV)
    expert_ids_turns = jax.random.permutation(jax.random.fold_in(splits[1], 3), DOMAINS * LENGTH // TOK_DEV)
    expert_ids = jax.vmap(lambda own, number: shared_out(jax.random.fold_in(splits[1], 2), own, number, TOK_DEV, EXPERTS, TOP, CAP, 2))(expert_ids_keys, expert_ids_turns).reshape((DOMAINS, LENGTH, TOP))
    attn_gain = jnp.clip(1.0 + 0.18 * jax.random.normal(splits[2], (D,), jnp.float32), 0.1, 1.9)
    w_query = centred(splits[3], (D, HEADS * HD), D ** -0.5, 0.1875, ((0, 64),))
    w_kv = centred(splits[4], (D, 2 * HD), D ** -0.5, 0.1875, ((0, 64),))
    w_out = centred(splits[5], (HEADS * HD, D), (HEADS * HD) ** -0.5, 0.1875, ((0, 64),))
    moe_gain = jnp.clip(1.0 + 0.18 * jax.random.normal(splits[6], (D,), jnp.float32), 0.1, 1.9)
    router = centred(splits[7], (D, EXPERTS), (D // 4) ** -0.5, 0.375)
    w_gate = centred(splits[8], (EXPERTS, D, EFF), D ** -0.5, 0.1875, ((0, 64), (2, 4)))
    w_up = centred(splits[9], (EXPERTS, D, EFF), D ** -0.5, 0.1875, ((0, 64), (2, 4)))
    w_down = centred(splits[10], (EXPERTS, EFF, D), (EFF // 4) ** -0.5, 0.1875, ((0, 64), (1, 4)))
    return dict(tokens=tokens, expert_ids=expert_ids, attn_gain=attn_gain, w_query=w_query, w_kv=w_kv, w_out=w_out, moe_gain=moe_gain, router=router, w_gate=w_gate, w_up=w_up, w_down=w_down)


epsilon = 1e-06

def rms_scaled(values):
    return values * lax.rsqrt(lax.optimization_barrier(jnp.mean(values * values, axis=-1, keepdims=True)) + epsilon)

def reference(tokens, expert_ids, attn_gain, w_query, w_kv, w_out, moe_gain, router, w_gate, w_up, w_down):
    floats = tokens.astype(jnp.float32)
    attn_in = (rms_scaled(floats) * attn_gain).astype(jnp.bfloat16)
    score_scale = HD ** (-0.5)

    def attend(sequence):
        queries = jnp.dot(sequence, w_query, preferred_element_type=jnp.float32).reshape(LENGTH, HEADS, HD)
        queries = rms_scaled(queries).astype(jnp.bfloat16).reshape(LENGTH * HEADS, HD)
        key_value = jnp.dot(sequence, w_kv, preferred_element_type=jnp.float32)
        keys = rms_scaled(key_value[:, :HD]).astype(jnp.bfloat16)
        values = key_value[:, HD:].astype(jnp.bfloat16)
        scores = jnp.dot(queries, keys.T, preferred_element_type=jnp.float32) * score_scale
        weights = jnp.exp(scores).astype(jnp.bfloat16)
        weighted = jnp.dot(weights, values, preferred_element_type=jnp.float32)
        totals = lax.optimization_barrier(jnp.sum(weights.astype(jnp.float32), axis=1, keepdims=True))
        context = (weighted / totals).astype(jnp.bfloat16).reshape(LENGTH, HEADS * HD)
        return jnp.dot(context, w_out, preferred_element_type=jnp.float32).astype(jnp.bfloat16)
    attention_out = lax.map(attend, attn_in)
    mixed_in = floats + attention_out.astype(jnp.float32)
    moe_in = (rms_scaled(mixed_in) * moe_gain).astype(jnp.bfloat16)
    flat_in = moe_in.reshape(-1, D)
    logits = jnp.dot(flat_in, router, preferred_element_type=jnp.float32)
    flat_ids = expert_ids.reshape(-1, TOP)
    chosen = jnp.take_along_axis(logits, flat_ids, axis=1)
    first = jax.nn.sigmoid(chosen[:, 0] - chosen[:, 1])
    blocks = DOMAINS * N_CTX
    block_ids = expert_ids.reshape(blocks, TOK_DEV * TOP)
    onehot = (block_ids[:, :, None] == jnp.arange(EXPERTS)[None, None, :]).astype(jnp.int32)
    earlier = jnp.cumsum(onehot, axis=1) - onehot
    slot = lax.optimization_barrier(jnp.sum(earlier * onehot, axis=2))
    column = (jnp.arange(blocks)[:, None] * CAP + slot).reshape(-1)
    expert = block_ids.reshape(-1)
    pair_rows = jnp.repeat(flat_in, TOP, axis=0)
    buffers = jnp.zeros((EXPERTS, blocks * CAP, D), jnp.bfloat16).at[expert, column].set(pair_rows)
    group_width = EFF // N_CTX

    def run_expert(operands):
        rows_in, gate_w, up_w, down_w = operands
        gated = jnp.dot(rows_in, gate_w, preferred_element_type=jnp.float32)
        lifted = jnp.dot(rows_in, up_w, preferred_element_type=jnp.float32)
        hidden = (jax.nn.silu(gated) * lifted).astype(jnp.bfloat16)
        total = jnp.zeros((rows_in.shape[0], D), jnp.float32)
        for group in range(N_CTX):
            term = jnp.dot(hidden[:, group * group_width:(group + 1) * group_width], down_w[group * group_width:(group + 1) * group_width], preferred_element_type=jnp.float32)
            total = total + lax.optimization_barrier(term.astype(jnp.bfloat16)).astype(jnp.float32)
        return total.astype(jnp.bfloat16)
    outputs = lax.map(run_expert, (buffers, w_gate, w_up, w_down))
    picked = outputs[expert, column].reshape(-1, TOP, D).astype(jnp.float32)
    mix = first[:, None] * picked[:, 0] + (1.0 - first)[:, None] * picked[:, 1]
    expert_mix = mix.astype(jnp.bfloat16).reshape(DOMAINS, LENGTH, D)
    return (attention_out, expert_mix)
```

```python
import functools

import jax
import jax.numpy as jnp
from jax import lax
from jax.experimental import pallas as pl
from jax.experimental.pallas import tpu as pltpu
from jax.sharding import PartitionSpec as P

HD = 128
TOP = 2
MESH = pl.DeviceIdType.MESH
NX, NY, NZ = 4, 4, 8


epsilon = 1e-06


def rms_scaled(values):
    return values * lax.rsqrt(jnp.mean(values * values, axis=-1, keepdims=True) + epsilon)


def here():
    ctx, exp = lax.axis_index("ctx"), lax.axis_index("exp")
    core, y = ctx % 2, exp % NY
    z, x_lo = (exp // NY) % NZ, exp // (NY * NZ)
    return (ctx // 2) * 2 + x_lo, y, z, core


def device(x, y, z, core):
    return (x // 2) * 2 + core, ((x % 2) * NZ + z) * NY + y


def signal(sem, target):
    pl.semaphore_signal(sem, inc=1, device_id=target, device_id_type=MESH)


CHUNKS = ((0, 0, 256), (0, 256, 256), (1, 0, 128), (2, 0, 256), (2, 256, 256))


def gather_kernel(q_in, kv_in, o_in, q_out, kv_out, o_out, own_sem, z_send, z_recv, y_send, y_recv, x_send, x_recv, s_send, s_recv):
    x, y, z, core = here()
    x_lo = x % 2
    ins, outs = (q_in, kv_in, o_in), (q_out, kv_out, o_out)
    barrier = pltpu.get_barrier_semaphore()
    partners = [device(x, y, (z + k) % NZ, core) for k in range(1, NZ)]
    partners += [device(x, (y + k) % NY, z, core) for k in range(1, NY)]
    partners += [device((x + k) % NX, y, z, core) for k in (1, 3)]
    partners += [device(x, y, z, 1 - core)]
    for partner in partners:
        signal(barrier, partner)

    def cols(chunk):
        array, first, width = CHUNKS[chunk]
        half = ins[array].shape[1] // 2
        return array, pl.ds(pl.multiple_of(core * half + first, 128), width)

    own = []
    for chunk in range(len(CHUNKS)):
        array, where = cols(chunk)
        copy = pltpu.make_async_copy(ins[array].at[:, where], outs[array].at[x_lo, z, y, :, where], own_sem.at[chunk])
        copy.start()
        own.append(copy)
    pl.semaphore_wait(barrier, len(partners))

    def remote(src, dst, send, recv, target):
        return pltpu.make_async_remote_copy(src_ref=src, dst_ref=dst, send_sem=send, recv_sem=recv, device_id=target, device_id_type=MESH)

    for chunk in range(len(CHUNKS)):
        array, where = cols(chunk)
        for k in (4, 3, 5, 2, 6, 1, 7):
            remote(ins[array].at[:, where], outs[array].at[x_lo, z, y, :, where], z_send.at[chunk], z_recv.at[chunk],
                   device(x, y, (z + k) % NZ, core)).start()

    def z_wait(chunk):
        array, where = cols(chunk)
        seven = outs[array].at[x_lo, pl.ds(0, NZ - 1), y, :, where]
        return remote(seven, seven, z_send.at[chunk], z_recv.at[chunk], partners[0])

    def y_step(chunk):
        array, where = cols(chunk)
        z_wait(chunk).wait_recv()
        own[chunk].wait()
        block = outs[array].at[x_lo, :, y, :, where]
        for k in (2, 1, 3):
            remote(block, block, y_send.at[chunk], y_recv.at[chunk], device(x, (y + k) % NY, z, core)).start()

    def y_wait(chunk):
        array, where = cols(chunk)
        three = outs[array].at[x_lo, :, pl.ds(0, NY - 1), :, where]
        return remote(three, three, y_send.at[chunk], y_recv.at[chunk], partners[0])

    def x_step(chunk):
        array, where = cols(chunk)
        y_wait(chunk).wait_recv()
        for k, first in ((1, 0), (3, NZ // 2)):
            part = outs[array].at[x_lo, pl.ds(first, NZ // 2), :, :, where]
            remote(part, part, x_send.at[chunk], x_recv.at[chunk], device((x + k) % NX, y, z, core)).start()
        part = outs[array].at[x_lo, :, :, :, where]
        remote(part, part, s_send.at[chunk], s_recv.at[chunk], device(x, y, z, 1 - core)).start()

    def x_wait(chunk):
        array, where = cols(chunk)
        mine, other = outs[array].at[x_lo, :, :, :, where], outs[array].at[1 - x_lo, :, :, :, where]
        return remote(mine, other, x_send.at[chunk], x_recv.at[chunk], partners[0])

    def s_step(chunk):
        array, where = cols(chunk)
        x_wait(chunk).wait_recv()
        part = outs[array].at[1 - x_lo, :, :, :, where]
        remote(part, part, s_send.at[chunk], s_recv.at[chunk], device(x, y, z, 1 - core)).start()

    n = len(CHUNKS)
    for step in range(n + 2):
        if step < n:
            y_step(step)
        if 0 <= step - 1 < n:
            x_step(step - 1)
        if 0 <= step - 2 < n:
            s_step(step - 2)
    for chunk in range(n):
        array, first, width = CHUNKS[chunk]
        half = ins[array].shape[1] // 2
        theirs = pl.ds(pl.multiple_of((1 - core) * half + first, 128), width)
        _, where = cols(chunk)
        both = remote(outs[array].at[:, :, :, :, where], outs[array].at[:, :, :, :, theirs], s_send.at[chunk], s_recv.at[chunk], partners[0])
        both.wait_recv()
        both.wait_send()
        z_wait(chunk).wait_send()
        y_wait(chunk).wait_send()
        x_wait(chunk).wait_send()


def gather_weights(*weights):
    n = len(CHUNKS)
    outs = pl.pallas_call(
        gather_kernel,
        out_shape=[jax.ShapeDtypeStruct((2, NZ, NY) + w.shape, w.dtype) for w in weights],
        in_specs=[pl.BlockSpec(memory_space=pl.ANY)] * 3,
        out_specs=[pl.BlockSpec(memory_space=pl.ANY)] * 3,
        scratch_shapes=[pltpu.SemaphoreType.DMA((n,))] * 9,
        compiler_params=pltpu.CompilerParams(collective_id=0, has_side_effects=True),
        name="gather_weights",
    )(*weights)
    return [o.reshape(-1, o.shape[-1]) for o in outs]


def body(
    tokens, expert_ids, attn_gain, w_query, w_kv, w_out, moe_gain, router, w_gate, w_up, w_down
):
    features = tokens.shape[-1]
    inputs = tokens.reshape(-1, features)
    tok_rows = inputs.shape[0]
    full_query, full_kv, full_out = gather_weights(w_query, w_kv, w_out)
    floats = inputs.astype(jnp.float32)
    attn_in = (rms_scaled(floats) * attn_gain).astype(jnp.bfloat16)
    head_count = full_query.shape[1] // HD
    queries = jnp.dot(attn_in, full_query, preferred_element_type=jnp.float32).reshape(
        tok_rows, head_count, HD
    )
    queries = rms_scaled(queries).astype(jnp.bfloat16).reshape(tok_rows * head_count, HD)
    key_value = jnp.dot(attn_in, full_kv, preferred_element_type=jnp.float32)
    keys = rms_scaled(key_value[:, :HD]).astype(jnp.bfloat16)
    values = key_value[:, HD:].astype(jnp.bfloat16)
    score_scale = HD ** (-0.5)
    key_piece = lax.all_gather(keys, "ctx", axis=0, tiled=True)
    value_piece = lax.all_gather(values, "ctx", axis=0, tiled=True)
    scores = (
        lax.dot_general(
            queries, key_piece, (((1,), (1,)), ((), ())), preferred_element_type=jnp.float32
        )
        * score_scale
    )
    weights = jnp.exp(scores).astype(jnp.bfloat16)
    weighted = jnp.dot(weights, value_piece, preferred_element_type=jnp.float32)
    totals = jnp.sum(weights.astype(jnp.float32), axis=1)
    weighted, totals = (weighted, totals)
    context = (weighted / totals[:, None]).astype(jnp.bfloat16).reshape(tok_rows, head_count * HD)
    attention_out = jnp.dot(context, full_out, preferred_element_type=jnp.float32).astype(
        jnp.bfloat16
    )
    mixed_in = floats + attention_out.astype(jnp.float32)
    moe_in = (rms_scaled(mixed_in) * moe_gain).astype(jnp.bfloat16)
    experts = router.shape[1]
    logits = jnp.dot(moe_in, router, preferred_element_type=jnp.float32)
    pair_ids = expert_ids.reshape(tok_rows, TOP)
    match = pair_ids[:, :, None] == jnp.arange(experts)[None, None, :]
    chosen = jnp.sum(jnp.where(match, logits[:, None, :], 0.0), axis=2)
    first = jax.nn.sigmoid(chosen[:, 0] - chosen[:, 1])
    gates = jnp.stack([first, 1.0 - first], axis=1)
    counts = match.reshape(tok_rows * TOP, experts).astype(jnp.int32)
    earlier = jnp.cumsum(counts, axis=0) - counts
    slot = jnp.sum(earlier * counts, axis=1)
    capacity = max(2, 3 * tok_rows * TOP // (2 * experts))
    position = slot * experts + pair_ids.reshape(-1)
    buffer = (
        jnp.zeros((capacity * experts, features), jnp.bfloat16)
        .at[position]
        .set(jnp.repeat(moe_in, TOP, axis=0))
    )
    received = lax.all_to_all(
        buffer.reshape(capacity, experts, features), "exp", split_axis=1, concat_axis=0, tiled=True
    )
    gathered = lax.all_gather(received, "ctx", axis=0, tiled=True)
    gated = jnp.einsum("red,edf->ref", gathered, w_gate, preferred_element_type=jnp.float32)
    lifted = jnp.einsum("red,edf->ref", gathered, w_up, preferred_element_type=jnp.float32)
    hidden = (jax.nn.silu(gated) * lifted).astype(jnp.bfloat16)
    summed = lax.psum_scatter(
        jnp.einsum("ref,efd->red", hidden, w_down, preferred_element_type=jnp.float32).astype(
            jnp.bfloat16
        ),
        "ctx",
        scatter_dimension=0,
        tiled=True,
    )
    returned = lax.all_to_all(summed, "exp", split_axis=0, concat_axis=1, tiled=True)
    picked = returned.reshape(capacity * experts, features)[position].reshape(
        tok_rows, TOP, features
    )
    expert_mix = jnp.sum(gates[:, :, None] * picked.astype(jnp.float32), axis=1).astype(
        jnp.bfloat16
    )
    return (attention_out.reshape(tokens.shape), expert_mix.reshape(tokens.shape))


def solution(mesh):
    in_specs = (
        P("exp", "ctx", None),
        P("exp", "ctx", None),
        P(),
        P("exp", None),
        P("exp", None),
        P("exp", None),
        P(),
        P(),
        P("exp", None, "ctx"),
        P("exp", None, "ctx"),
        P("exp", "ctx", None),
    )
    out_specs = (P("exp", "ctx", None), P("exp", "ctx", None))
    return jax.shard_map(body, mesh=mesh, in_specs=in_specs, out_specs=out_specs, check_vma=False)
```

```python
import functools

import jax
import jax.numpy as jnp
from jax import lax
from jax.experimental import pallas as pl
from jax.experimental.pallas import tpu as pltpu
from jax.sharding import PartitionSpec as P

HD = 128
TOP = 2
MESH = pl.DeviceIdType.MESH
NX, NY, NZ = 4, 4, 8


epsilon = 1e-06


def rms_scaled(values):
    return values * lax.rsqrt(jnp.mean(values * values, axis=-1, keepdims=True) + epsilon)


def here():
    ctx, exp = lax.axis_index("ctx"), lax.axis_index("exp")
    core, y = ctx % 2, exp % NY
    z, x_lo = (exp // NY) % NZ, exp // (NY * NZ)
    return (ctx // 2) * 2 + x_lo, y, z, core


def device(x, y, z, core):
    return (x // 2) * 2 + core, ((x % 2) * NZ + z) * NY + y


def signal(sem, target):
    pl.semaphore_signal(sem, inc=1, device_id=target, device_id_type=MESH)


CHUNKS = ((0, 0, 256), (0, 256, 256), (1, 0, 128), (2, 0, 256), (2, 256, 256))


def gather_kernel(q_in, kv_in, o_in, q_out, kv_out, o_out, own_sem, z_send, z_recv, y_send, y_recv, x_send, x_recv, s_send, s_recv):
    x, y, z, core = here()
    x_lo = x % 2
    ins, outs = (q_in, kv_in, o_in), (q_out, kv_out, o_out)
    barrier = pltpu.get_barrier_semaphore()
    partners = [device(x, y, (z + k) % NZ, core) for k in range(1, NZ)]
    partners += [device(x, (y + k) % NY, z, core) for k in range(1, NY)]
    partners += [device((x + k) % NX, y, z, core) for k in (1, 3)]
    partners += [device(x, y, z, 1 - core)]
    for partner in partners:
        signal(barrier, partner)

    def cols(chunk):
        array, first, width = CHUNKS[chunk]
        half = ins[array].shape[1] // 2
        return array, pl.ds(pl.multiple_of(core * half + first, 128), width)

    own = []
    for chunk in range(len(CHUNKS)):
        array, where = cols(chunk)
        copy = pltpu.make_async_copy(ins[array].at[:, where], outs[array].at[x_lo, z, y, :, where], own_sem.at[chunk])
        copy.start()
        own.append(copy)
    pl.semaphore_wait(barrier, len(partners))

    def remote(src, dst, send, recv, target):
        return pltpu.make_async_remote_copy(src_ref=src, dst_ref=dst, send_sem=send, recv_sem=recv, device_id=target, device_id_type=MESH)

    for chunk in range(len(CHUNKS)):
        array, where = cols(chunk)
        for k in (4, 3, 5, 2, 6, 1, 7):
            remote(ins[array].at[:, where], outs[array].at[x_lo, z, y, :, where], z_send.at[chunk], z_recv.at[chunk],
                   device(x, y, (z + k) % NZ, core)).start()

    def z_wait(chunk):
        array, where = cols(chunk)
        seven = outs[array].at[x_lo, pl.ds(0, NZ - 1), y, :, where]
        return remote(seven, seven, z_send.at[chunk], z_recv.at[chunk], partners[0])

    def y_step(chunk):
        array, where = cols(chunk)
        z_wait(chunk).wait_recv()
        own[chunk].wait()
        block = outs[array].at[x_lo, :, y, :, where]
        for k in (2, 1, 3):
            remote(block, block, y_send.at[chunk], y_recv.at[chunk], device(x, (y + k) % NY, z, core)).start()

    def y_wait(chunk):
        array, where = cols(chunk)
        three = outs[array].at[x_lo, :, pl.ds(0, NY - 1), :, where]
        return remote(three, three, y_send.at[chunk], y_recv.at[chunk], partners[0])

    def x_step(chunk):
        array, where = cols(chunk)
        y_wait(chunk).wait_recv()
        for k, first in ((1, 0), (3, NZ // 2)):
            part = outs[array].at[x_lo, pl.ds(first, NZ // 2), :, :, where]
            remote(part, part, x_send.at[chunk], x_recv.at[chunk], device((x + k) % NX, y, z, core)).start()
        part = outs[array].at[x_lo, :, :, :, where]
        remote(part, part, s_send.at[chunk], s_recv.at[chunk], device(x, y, z, 1 - core)).start()

    def x_wait(chunk):
        array, where = cols(chunk)
        mine, other = outs[array].at[x_lo, :, :, :, where], outs[array].at[1 - x_lo, :, :, :, where]
        return remote(mine, other, x_send.at[chunk], x_recv.at[chunk], partners[0])

    def s_step(chunk):
        array, where = cols(chunk)
        x_wait(chunk).wait_recv()
        part = outs[array].at[1 - x_lo, :, :, :, where]
        remote(part, part, s_send.at[chunk], s_recv.at[chunk], device(x, y, z, 1 - core)).start()

    n = len(CHUNKS)
    for step in range(n + 2):
        if step < n:
            y_step(step)
        if 0 <= step - 1 < n:
            x_step(step - 1)
        if 0 <= step - 2 < n:
            s_step(step - 2)
    for chunk in range(n):
        array, first, width = CHUNKS[chunk]
        half = ins[array].shape[1] // 2
        theirs = pl.ds(pl.multiple_of((1 - core) * half + first, 128), width)
        _, where = cols(chunk)
        both = remote(outs[array].at[:, :, :, :, where], outs[array].at[:, :, :, :, theirs], s_send.at[chunk], s_recv.at[chunk], partners[0])
        both.wait_recv()
        both.wait_send()
        z_wait(chunk).wait_send()
        y_wait(chunk).wait_send()
        x_wait(chunk).wait_send()


def gather_weights(*weights):
    n = len(CHUNKS)
    outs = pl.pallas_call(
        gather_kernel,
        out_shape=[jax.ShapeDtypeStruct((2, NZ, NY) + w.shape, w.dtype) for w in weights],
        in_specs=[pl.BlockSpec(memory_space=pl.ANY)] * 3,
        out_specs=[pl.BlockSpec(memory_space=pl.ANY)] * 3,
        scratch_shapes=[pltpu.SemaphoreType.DMA((n,))] * 9,
        compiler_params=pltpu.CompilerParams(collective_id=0, has_side_effects=True),
        name="gather_weights",
    )(*weights)
    return [o.reshape(-1, o.shape[-1]) for o in outs]


CAP = 6
DRAIN = 256


def expert_kernel(pos_ref, pair_ref, gate_ref, moe_ref, wg_hbm, wu_hbm, wd_hbm, out_ref,
                  wg, wu, wd, sent, came, rows, hidden, terms, theirs, halves, sides, final, back,
                  w_sem, zy_send, zy_recv, x_send, x_recv, s_send, s_recv, own_sem,
                  rs_send, rs_recv, rx_send, rx_recv, rz_send, rz_recv):
    x, y, z, core = here()
    x_lo = x % 2
    features = moe_ref.shape[1]
    block = NZ * CAP
    barrier = pltpu.get_barrier_semaphore()
    plane = [(k, d) for d in (0, 1, 3, 2) for k in (4, 3, 5, 2, 6, 1, 7, 0) if (k, d) != (0, 0)]
    sibling = device(x, y, z, 1 - core)
    partners = [device(x, (y + d) % NY, (z + k) % NZ, core) for k, d in plane]
    partners += [device((x + k) % NX, y, z, core) for k in range(1, NX)] + [sibling]
    for partner in partners:
        signal(barrier, partner)
    loads = [pltpu.make_async_copy(src.at[0], dst, w_sem.at[i]) for i, (src, dst) in enumerate(((wg_hbm, wg), (wu_hbm, wu), (wd_hbm, wd)))]
    for load in loads:
        load.start()

    def remote(src, dst, send, recv, target):
        return pltpu.make_async_remote_copy(src_ref=src, dst_ref=dst, send_sem=send, recv_sem=recv, device_id=target, device_id_type=MESH)

    def local(src, dst, sem):
        return pltpu.make_async_copy(src, dst, sem)

    row = lax.broadcasted_iota(jnp.int32, (2 * NZ * NY * CAP, pos_ref.shape[1]), 0)
    chosen = jnp.where((row == pos_ref[0:1, :]) | (row == pos_ref[1:2, :]), 1.0, 0.0).astype(jnp.bfloat16)
    sent[...] = jnp.dot(chosen, moe_ref[...], preferred_element_type=jnp.float32).astype(jnp.bfloat16).reshape(sent.shape)
    pl.semaphore_wait(barrier, len(partners))

    for k, d in plane:
        to_z, to_y = (z + k) % NZ, (y + d) % NY
        remote(sent.at[to_z, to_y], came.at[d, z], zy_send, zy_recv.at[d], device(x, to_y, to_z, core)).start()
    own = local(sent.at[z, y], came.at[0, z], own_sem.at[0])
    own.start()

    def zy_wait(d):
        count = NZ if d else NZ - 1
        return remote(came.at[d, pl.ds(0, count)], came.at[d, pl.ds(0, count)], zy_send, zy_recv.at[d], sibling)

    def spread(d):
        zy_wait(d).wait_recv()
        if d == 0:
            own.wait()
        for k, part in ((2, x_lo), (1, 1 - x_lo), (3, 1 - x_lo)):
            remote(came.at[d, :, part], rows.at[d, core, k - 1], x_send.at[d], x_recv.at[d], device((x + k) % NX, y, z, core)).start()
        local(came.at[d, :, x_lo], rows.at[d, core, 3], own_sem.at[1 + d]).start()
        remote(came.at[d, :, x_lo], rows.at[d, core, 3], s_send.at[d], s_recv.at[d], sibling).start()

    def x_wait(d):
        three = rows.at[d, core, pl.ds(0, 3)]
        return remote(three, three, x_send.at[d], x_recv.at[d], sibling)

    def share(d):
        x_wait(d).wait_recv()
        three = rows.at[d, core, pl.ds(0, 3)]
        remote(three, three, s_send.at[d], s_recv.at[d], sibling).start()

    def s_wait(d):
        return remote(rows.at[d, core], rows.at[d, 1 - core], s_send.at[d], s_recv.at[d], sibling)

    def compute(d):
        s_wait(d).wait_recv()
        local(came.at[d, :, x_lo], rows.at[d, core, 3], own_sem.at[1 + d]).wait()
        if d == 0:
            for load in loads:
                load.wait()
        many = rows[d].reshape(2 * NX * block, features)

        def up(tile, carry):
            where = pl.ds(pl.multiple_of(tile * DRAIN, DRAIN), DRAIN)
            gated = jnp.dot(many, wg[:, where], preferred_element_type=jnp.float32)
            lifted = jnp.dot(many, wu[:, where], preferred_element_type=jnp.float32)
            hidden[:, where] = (gated / (1.0 + jnp.exp(-gated)) * lifted).astype(jnp.bfloat16)
            return carry

        lax.fori_loop(0, wg.shape[1] // DRAIN, up, 0)
        inner = hidden[...]

        def down(tile, carry):
            where = pl.ds(pl.multiple_of(tile * DRAIN, DRAIN), DRAIN)
            term = jnp.dot(inner, wd[:, where], preferred_element_type=jnp.float32).astype(jnp.bfloat16)
            terms[d, :, :, :, :, where] = term.reshape(2, NX, NZ, CAP, DRAIN)
            return carry

        lax.fori_loop(0, features // DRAIN, down, 0)
        remote(terms.at[d, 1 - core], theirs.at[d], rs_send.at[d], rs_recv.at[d], sibling).start()

    def rs_wait(d):
        return remote(terms.at[d, 1 - core], theirs.at[d], rs_send.at[d], rs_recv.at[d], sibling)

    def halve(d):
        rs_wait(d).wait_recv()
        halves[d] = (terms[d, core].astype(jnp.float32) + theirs[d].astype(jnp.float32)).astype(jnp.bfloat16)
        for k in (2, 1, 3):
            remote(halves.at[d, k - 1], sides.at[d, k - 1], rx_send.at[d], rx_recv.at[d], device((x - k + NX) % NX, y, z, core)).start()

    def rx_wait(d):
        return remote(halves.at[d, pl.ds(0, 3)], sides.at[d], rx_send.at[d], rx_recv.at[d], sibling)

    def finish(d):
        rx_wait(d).wait_recv()
        final[d, :, x_lo] = (halves[d, 3].astype(jnp.float32) + sides[d, 1].astype(jnp.float32)).astype(jnp.bfloat16)
        final[d, :, 1 - x_lo] = (sides[d, 0].astype(jnp.float32) + sides[d, 2].astype(jnp.float32)).astype(jnp.bfloat16)
        for k in (4, 3, 5, 2, 6, 1, 7, 0):
            if (k, d) == (0, 0):
                local(final.at[d, z], back.at[y, z], own_sem.at[1 + NY]).start()
            else:
                to_z, to_y = (z + k) % NZ, (y - d + NY) % NY
                remote(final.at[d, to_z], back.at[y, z], rz_send, rz_recv.at[d], device(x, to_y, to_z, core)).start()

    def pick(d):
        count, from_y = NZ if d else NZ - 1, (y + d) % NY
        part = back.at[from_y, pl.ds(0, count)]
        remote(part, part, rz_send, rz_recv.at[d], sibling).wait_recv()
        if d == 0:
            local(final.at[d, z], back.at[y, z], own_sem.at[1 + NY]).wait()
        tokens = pair_ref.shape[0]
        place = lax.broadcasted_iota(jnp.int32, (tokens, 2 * block), 1) + from_y * (2 * block)
        got = back[from_y].reshape(2 * block, features)
        total = None
        for choice in range(TOP):
            mine = jnp.where(place == pair_ref[:, choice:choice + 1], 1.0, 0.0).astype(jnp.bfloat16)
            part = gate_ref[:, choice:choice + 1] * jnp.dot(mine, got, preferred_element_type=jnp.float32)
            total = part if total is None else total + part
        return total

    spread(0)
    spread(1)
    share(0)
    compute(0)
    spread(3)
    share(1)
    compute(1)
    halve(0)
    spread(2)
    share(3)
    compute(3)
    halve(1)
    finish(0)
    share(2)
    compute(2)
    halve(3)
    finish(1)
    halve(2)
    finish(3)
    finish(2)
    total = pick(0) + pick(1)
    total = total + pick(3)
    total = total + pick(2)
    out_ref[...] = total.astype(out_ref.dtype)

    for d in range(NY):
        x_wait(d).wait_send()
        s_wait(d).wait_send()
        rs_wait(d).wait_send()
        rx_wait(d).wait_send()
    for sent_ref, sem in ((came, zy_send), (final, rz_send)):
        some = sent_ref.at[pl.ds(0, NY - 1)]
        remote(some, some, sem, zy_recv.at[0], sibling).wait_send()
        rest = sent_ref.at[0, pl.ds(0, NZ - 1)]
        remote(rest, rest, sem, zy_recv.at[0], sibling).wait_send()


def run_experts(pos, pair, gates, moe_in, w_gate, w_up, w_down):
    tokens, features = moe_in.shape
    width = w_gate.shape[2]
    bf16, f32 = jnp.bfloat16, jnp.float32
    block = (NZ, CAP, features)
    dma, vmem = pltpu.SemaphoreType.DMA, pltpu.VMEM
    return pl.pallas_call(
        expert_kernel,
        out_shape=jax.ShapeDtypeStruct((tokens, features), bf16),
        in_specs=[pl.BlockSpec(memory_space=vmem)] * 4 + [pl.BlockSpec(memory_space=pl.ANY)] * 3,
        out_specs=pl.BlockSpec(memory_space=vmem),
        scratch_shapes=[
            vmem((features, width), bf16),
            vmem((features, width), bf16),
            vmem((width, features), bf16),
            vmem((NZ, NY, 2, CAP, features), bf16),
            vmem((NY, NZ, 2, CAP, features), bf16),
            vmem((NY, 2, NX) + block, bf16),
            vmem((2 * NX * NZ * CAP, width), bf16),
            vmem((NY, 2, NX) + block, bf16),
            vmem((NY, NX) + block, bf16),
            vmem((NY, NX) + block, bf16),
            vmem((NY, NX - 1) + block, bf16),
            vmem((NY, NZ, 2, CAP, features), bf16),
            vmem((NY, NZ, 2, CAP, features), bf16),
            dma((3,)), dma, dma((NY,)), dma((NY,)), dma((NY,)), dma((NY,)), dma((NY,)), dma((2 + NY,)),
            dma((NY,)), dma((NY,)), dma((NY,)), dma((NY,)), dma, dma((NY,)),
        ],
        compiler_params=pltpu.CompilerParams(collective_id=1, has_side_effects=True, vmem_limit_bytes=60 << 20),
        name="run_experts",
    )(pos, pair, gates, moe_in, w_gate, w_up, w_down)


def body(
    tokens, expert_ids, attn_gain, w_query, w_kv, w_out, moe_gain, router, w_gate, w_up, w_down
):
    features = tokens.shape[-1]
    inputs = tokens.reshape(-1, features)
    tok_rows = inputs.shape[0]
    full_query, full_kv, full_out = gather_weights(w_query, w_kv, w_out)
    floats = inputs.astype(jnp.float32)
    attn_in = (rms_scaled(floats) * attn_gain).astype(jnp.bfloat16)
    head_count = full_query.shape[1] // HD
    queries = jnp.dot(attn_in, full_query, preferred_element_type=jnp.float32).reshape(
        tok_rows, head_count, HD
    )
    queries = rms_scaled(queries).astype(jnp.bfloat16).reshape(tok_rows * head_count, HD)
    key_value = jnp.dot(attn_in, full_kv, preferred_element_type=jnp.float32)
    keys = rms_scaled(key_value[:, :HD]).astype(jnp.bfloat16)
    values = key_value[:, HD:].astype(jnp.bfloat16)
    score_scale = HD ** (-0.5)
    key_piece = lax.all_gather(keys, "ctx", axis=0, tiled=True)
    value_piece = lax.all_gather(values, "ctx", axis=0, tiled=True)
    scores = (
        lax.dot_general(
            queries, key_piece, (((1,), (1,)), ((), ())), preferred_element_type=jnp.float32
        )
        * score_scale
    )
    weights = jnp.exp(scores).astype(jnp.bfloat16)
    weighted = jnp.dot(weights, value_piece, preferred_element_type=jnp.float32)
    totals = jnp.sum(weights.astype(jnp.float32), axis=1)
    weighted, totals = (weighted, totals)
    context = (weighted / totals[:, None]).astype(jnp.bfloat16).reshape(tok_rows, head_count * HD)
    attention_out = jnp.dot(context, full_out, preferred_element_type=jnp.float32).astype(
        jnp.bfloat16
    )
    mixed_in = floats + attention_out.astype(jnp.float32)
    moe_in = (rms_scaled(mixed_in) * moe_gain).astype(jnp.bfloat16)
    experts = router.shape[1]
    logits = jnp.dot(moe_in, router, preferred_element_type=jnp.float32)
    pair_ids = expert_ids.reshape(tok_rows, TOP)
    match = pair_ids[:, :, None] == jnp.arange(experts)[None, None, :]
    chosen = jnp.sum(jnp.where(match, logits[:, None, :], 0.0), axis=2)
    first = jax.nn.sigmoid(chosen[:, 0] - chosen[:, 1])
    gates = jnp.stack([first, 1.0 - first], axis=1)
    counts = match.reshape(tok_rows * TOP, experts).astype(jnp.int32)
    earlier = jnp.cumsum(counts, axis=0) - counts
    slot = jnp.sum(earlier * counts, axis=1).reshape(tok_rows, TOP)
    chip = pair_ids % (NZ * NY)
    sent_place = (chip * 2 + pair_ids // (NZ * NY)) * CAP + slot
    back_place = (((chip % NY) * NZ + chip // NY) * 2 + pair_ids // (NZ * NY)) * CAP + slot
    expert_mix = run_experts(sent_place.T, back_place, gates, moe_in, w_gate, w_up, w_down)
    return (attention_out.reshape(tokens.shape), expert_mix.reshape(tokens.shape))


def solution(mesh):
    in_specs = (
        P("exp", "ctx", None),
        P("exp", "ctx", None),
        P(),
        P("exp", None),
        P("exp", None),
        P("exp", None),
        P(),
        P(),
        P("exp", None, "ctx"),
        P("exp", None, "ctx"),
        P("exp", "ctx", None),
    )
    out_specs = (P("exp", "ctx", None), P("exp", "ctx", None))
    return jax.shard_map(body, mesh=mesh, in_specs=in_specs, out_specs=out_specs, check_vma=False)
```

```python
import functools

import jax
import jax.numpy as jnp
from jax import lax
from jax.experimental import pallas as pl
from jax.experimental.pallas import tpu as pltpu
from jax.sharding import PartitionSpec as P

HD = 128
TOP = 2
MESH = pl.DeviceIdType.MESH
NX, NY, NZ = 4, 4, 8


epsilon = 1e-06
bf16, f32 = jnp.bfloat16, jnp.float32


def rms_scaled(values):
    return values * lax.rsqrt(jnp.mean(values * values, axis=-1, keepdims=True) + epsilon)


def here():
    ctx, exp = lax.axis_index("ctx"), lax.axis_index("exp")
    core, y = ctx % 2, exp % NY
    z, x_lo = (exp // NY) % NZ, exp // (NY * NZ)
    return (ctx // 2) * 2 + x_lo, y, z, core


def device(x, y, z, core):
    return (x // 2) * 2 + core, ((x % 2) * NZ + z) * NY + y


def signal(sem, target):
    pl.semaphore_signal(sem, inc=1, device_id=target, device_id_type=MESH)


CHUNKS = ((1, 0, 128), (0, 0, 256), (0, 256, 256), (2, 0, 256), (2, 256, 256))
TILE = 256
CAP = 6
DRAIN = 256


def remote(src, dst, send, recv, target):
    return pltpu.make_async_remote_copy(src_ref=src, dst_ref=dst, send_sem=send, recv_sem=recv, device_id=target, device_id_type=MESH)


def local(src, dst, sem):
    return pltpu.make_async_copy(src, dst, sem)


def layer_kernel(tok_ref, id_ref, again_ref, mgain_ref, router_ref, q_in, kv_in, o_in, wg_hbm, wu_hbm, wd_hbm, att_ref, mix_ref,
                 q_all, kv_all, o_all, normed, queries, key_values, context, moe_ref, chosen_ref, back_ref, gate_ref,
                 wg, wu, wd, sent, came, rows, hidden, terms, theirs, halves, sides, final, back,
                 g_own, z_send, z_recv, y_send, y_recv, gx_send, gx_recv, gs_send, gs_recv, kv_send, kv_recv,
                 w_sem, zy_send, zy_recv, x_send, x_recv, s_send, s_recv, own_sem,
                 rs_send, rs_recv, rx_send, rx_recv, rz_send, rz_recv):
    x, y, z, core = here()
    x_lo = x % 2
    features = tok_ref.shape[2]
    tokens = tok_ref.shape[1]
    experts = router_ref.shape[1]
    block = NZ * CAP
    plane = [(k, d) for d in (0, 1, 3, 2) for k in (4, 3, 5, 2, 6, 1, 7, 0) if (k, d) != (0, 0)]
    sibling = device(x, y, z, 1 - core)
    barrier = pltpu.get_barrier_semaphore()
    partners = [device(x, (y + d) % NY, (z + k) % NZ, core) for k, d in plane]
    partners += [device((x + k) % NX, y, z, core) for k in range(1, NX)]
    partners += [sibling, device((x + 2) % NX, y, z, 1 - core)]
    for partner in partners:
        signal(barrier, partner)

    ins, outs = (q_in, kv_in, o_in), (q_all, kv_all, o_all)

    def cols(chunk):
        array, first, width = CHUNKS[chunk]
        half = ins[array].shape[1] // 2
        return array, pl.ds(pl.multiple_of(core * half + first, 128), width)

    own = []
    for chunk in range(len(CHUNKS)):
        array, where = cols(chunk)
        copy = local(ins[array].at[:, where], outs[array].at[x_lo, z, y, :, where], g_own.at[chunk])
        copy.start()
        own.append(copy)
    pl.semaphore_wait(barrier, len(partners))
    for chunk in range(len(CHUNKS)):
        array, where = cols(chunk)
        for k in (4, 3, 5, 2, 6, 1, 7):
            remote(ins[array].at[:, where], outs[array].at[x_lo, z, y, :, where], z_send.at[chunk], z_recv.at[chunk],
                   device(x, y, (z + k) % NZ, core)).start()

    def z_wait(chunk):
        array, where = cols(chunk)
        seven = outs[array].at[x_lo, pl.ds(0, NZ - 1), y, :, where]
        return remote(seven, seven, z_send.at[chunk], z_recv.at[chunk], sibling)

    def y_step(chunk):
        array, where = cols(chunk)
        z_wait(chunk).wait_recv()
        own[chunk].wait()
        part = outs[array].at[x_lo, :, y, :, where]
        for k in (2, 1, 3):
            remote(part, part, y_send.at[chunk], y_recv.at[chunk], device(x, (y + k) % NY, z, core)).start()

    def y_wait(chunk):
        array, where = cols(chunk)
        three = outs[array].at[x_lo, :, pl.ds(0, NY - 1), :, where]
        return remote(three, three, y_send.at[chunk], y_recv.at[chunk], sibling)

    def x_step(chunk):
        array, where = cols(chunk)
        y_wait(chunk).wait_recv()
        for k, first in ((1, 0), (3, NZ // 2)):
            part = outs[array].at[x_lo, pl.ds(first, NZ // 2), :, :, where]
            remote(part, part, gx_send.at[chunk], gx_recv.at[chunk], device((x + k) % NX, y, z, core)).start()
        part = outs[array].at[x_lo, :, :, :, where]
        remote(part, part, gs_send.at[chunk], gs_recv.at[chunk], sibling).start()

    def gx_wait(chunk):
        array, where = cols(chunk)
        mine, other = outs[array].at[x_lo, :, :, :, where], outs[array].at[1 - x_lo, :, :, :, where]
        return remote(mine, other, gx_send.at[chunk], gx_recv.at[chunk], sibling)

    def gs_step(chunk):
        array, where = cols(chunk)
        gx_wait(chunk).wait_recv()
        part = outs[array].at[1 - x_lo, :, :, :, where]
        remote(part, part, gs_send.at[chunk], gs_recv.at[chunk], sibling).start()

    def gs_wait(chunk):
        array, first, width = CHUNKS[chunk]
        half = ins[array].shape[1] // 2
        theirs_at = pl.ds(pl.multiple_of((1 - core) * half + first, 128), width)
        _, where = cols(chunk)
        return remote(outs[array].at[:, :, :, :, where], outs[array].at[:, :, :, :, theirs_at], gs_send.at[chunk], gs_recv.at[chunk], sibling)

    floats = tok_ref[0].astype(f32)
    normed[...] = (rms_scaled(floats) * again_ref[...]).astype(bf16)
    lane = lax.broadcasted_iota(jnp.int32, (tokens, experts), 1)
    named = [id_ref[0, :, choice:choice + 1] == lane for choice in range(TOP)]
    either = jnp.where(named[0] | named[1], 1.0, 0.0).astype(bf16)
    down, across = (lax.broadcasted_iota(jnp.int32, (tokens, tokens), i) for i in (0, 1))
    before = jnp.dot(jnp.where(across < down, 1.0, 0.0).astype(bf16), either, preferred_element_type=f32)
    sent_at = []
    for choice in range(TOP):
        slot = jnp.sum(jnp.where(named[choice], before, 0.0), axis=1, keepdims=True).astype(jnp.int32)
        expert = id_ref[0, :, choice:choice + 1]
        chip, low = expert % (NZ * NY), expert // (NZ * NY)
        back_ref[:, choice:choice + 1] = (((chip % NY) * NZ + chip // NY) * 2 + low) * CAP + slot
        place = ((chip * 2 + low) * CAP + slot).astype(f32)
        sent_at.append(jnp.sum(jnp.where(across == down, place, 0.0), axis=0, keepdims=True).astype(jnp.int32))
    row = lax.broadcasted_iota(jnp.int32, (2 * NZ * NY * CAP, tokens), 0)
    chosen_ref[...] = jnp.where((row == sent_at[0]) | (row == sent_at[1]), 1.0, 0.0).astype(bf16)
    loads = [local(src.at[0], dst, w_sem.at[i]) for i, (src, dst) in enumerate(((wg_hbm, wg), (wu_hbm, wu), (wd_hbm, wd)))]

    def matrix(ref, tile):
        return ref[:, :, :, :, tile * TILE:(tile + 1) * TILE].reshape(-1, TILE)

    ctx = (x // 2) * 2 + core
    peers = [device((x + 2) % NX, y, z, core), sibling, device((x + 2) % NX, y, z, 1 - core)]

    def make_keys():
        pair = jnp.dot(normed[...], matrix(kv_all, 0), preferred_element_type=f32)
        key_values[ctx, :, :HD] = rms_scaled(pair[:, :HD]).astype(bf16)
        key_values[ctx, :, HD:] = pair[:, HD:].astype(bf16)
        for peer in peers:
            remote(key_values.at[ctx], key_values.at[ctx], kv_send, kv_recv, peer).start()

    def kv_wait():
        three = key_values.at[pl.ds(0, 3)]
        return remote(three, three, kv_send, kv_recv, sibling)

    def make_queries(tile):
        wide = jnp.dot(normed[...], matrix(q_all, tile), preferred_element_type=f32)
        for head in range(TILE // HD):
            queries[tile * 2 + head] = rms_scaled(wide[:, head * HD:(head + 1) * HD]).astype(bf16)

    def attend(tile):
        keys = key_values[:, :, :HD].reshape(-1, HD)
        values = key_values[:, :, HD:].reshape(-1, HD)
        for head in (tile * 2, tile * 2 + 1):
            scores = lax.dot_general(queries[head], keys, (((1,), (1,)), ((), ())), preferred_element_type=f32) * (HD ** (-0.5))
            weights = jnp.exp(scores).astype(bf16)
            weighted = jnp.dot(weights, values, preferred_element_type=f32)
            totals = jnp.sum(weights.astype(f32), axis=1, keepdims=True)
            context[:, head * HD:(head + 1) * HD] = (weighted / totals).astype(bf16)

    def project(tile):
        att_ref[0, :, tile * TILE:(tile + 1) * TILE] = jnp.dot(context[...], matrix(o_all, tile), preferred_element_type=f32).astype(bf16)

    y_step(0)
    y_step(1)
    x_step(0)
    y_step(2)
    x_step(1)
    gs_step(0)
    gs_wait(0).wait_recv()
    make_keys()
    y_step(3)
    x_step(2)
    gs_step(1)
    gs_wait(1).wait_recv()
    make_queries(0)
    make_queries(2)
    y_step(4)
    x_step(3)
    gs_step(2)
    gs_wait(2).wait_recv()
    make_queries(1)
    make_queries(3)
    kv_wait().wait_recv()
    attend(0)
    x_step(4)
    attend(1)
    gs_step(3)
    attend(2)
    attend(3)
    gs_step(4)
    for load in loads:
        load.start()
    gs_wait(3).wait_recv()
    project(0)
    project(2)
    gs_wait(4).wait_recv()
    project(1)
    project(3)
    mixed = floats + att_ref[0].astype(f32)
    moe_ref[...] = (rms_scaled(mixed) * mgain_ref[...]).astype(bf16)

    sent[...] = jnp.dot(chosen_ref[...], moe_ref[...], preferred_element_type=f32).astype(bf16).reshape(sent.shape)
    for k, d in plane:
        to_z, to_y = (z + k) % NZ, (y + d) % NY
        remote(sent.at[to_z, to_y], came.at[d, z], zy_send, zy_recv.at[d], device(x, to_y, to_z, core)).start()
    own_block = local(sent.at[z, y], came.at[0, z], own_sem.at[0])
    own_block.start()
    logits = jnp.dot(moe_ref[...], router_ref[...], preferred_element_type=f32)
    picked = [jnp.sum(jnp.where(id_ref[0, :, choice:choice + 1] == lane, logits, 0.0), axis=1, keepdims=True) for choice in range(TOP)]
    first = jax.nn.sigmoid(picked[0] - picked[1])
    gate_ref[:, 0:1] = first
    gate_ref[:, 1:2] = 1.0 - first

    def zy_wait(d):
        count = NZ if d else NZ - 1
        return remote(came.at[d, pl.ds(0, count)], came.at[d, pl.ds(0, count)], zy_send, zy_recv.at[d], sibling)

    def spread(d):
        zy_wait(d).wait_recv()
        if d == 0:
            own_block.wait()
        for k, part in ((2, x_lo), (1, 1 - x_lo), (3, 1 - x_lo)):
            remote(came.at[d, :, part], rows.at[d, core, k - 1], x_send.at[d], x_recv.at[d], device((x + k) % NX, y, z, core)).start()
        local(came.at[d, :, x_lo], rows.at[d, core, 3], own_sem.at[1 + d]).start()
        remote(came.at[d, :, x_lo], rows.at[d, core, 3], s_send.at[d], s_recv.at[d], sibling).start()

    def x_wait(d):
        three = rows.at[d, core, pl.ds(0, 3)]
        return remote(three, three, x_send.at[d], x_recv.at[d], sibling)

    def share(d):
        x_wait(d).wait_recv()
        three = rows.at[d, core, pl.ds(0, 3)]
        remote(three, three, s_send.at[d], s_recv.at[d], sibling).start()

    def s_wait(d):
        return remote(rows.at[d, core], rows.at[d, 1 - core], s_send.at[d], s_recv.at[d], sibling)

    def compute(d):
        s_wait(d).wait_recv()
        local(came.at[d, :, x_lo], rows.at[d, core, 3], own_sem.at[1 + d]).wait()
        if d == 0:
            for load in loads:
                load.wait()
        many = rows[d].reshape(2 * NX * block, features)

        def up(tile, carry):
            where = pl.ds(pl.multiple_of(tile * DRAIN, DRAIN), DRAIN)
            gated = jnp.dot(many, wg[:, where], preferred_element_type=f32)
            lifted = jnp.dot(many, wu[:, where], preferred_element_type=f32)
            hidden[:, where] = (gated / (1.0 + jnp.exp(-gated)) * lifted).astype(bf16)
            return carry

        lax.fori_loop(0, wg.shape[1] // DRAIN, up, 0)
        inner = hidden[...]

        def down(tile, carry):
            where = pl.ds(pl.multiple_of(tile * DRAIN, DRAIN), DRAIN)
            term = jnp.dot(inner, wd[:, where], preferred_element_type=f32).astype(bf16)
            terms[d, :, :, :, :, where] = term.reshape(2, NX, NZ, CAP, DRAIN)
            return carry

        lax.fori_loop(0, features // DRAIN, down, 0)
        remote(terms.at[d, 1 - core], theirs.at[d], rs_send.at[d], rs_recv.at[d], sibling).start()

    def rs_wait(d):
        return remote(terms.at[d, 1 - core], theirs.at[d], rs_send.at[d], rs_recv.at[d], sibling)

    def halve(d):
        rs_wait(d).wait_recv()
        halves[d] = (terms[d, core].astype(f32) + theirs[d].astype(f32)).astype(bf16)
        for k in (2, 1, 3):
            remote(halves.at[d, k - 1], sides.at[d, k - 1], rx_send.at[d], rx_recv.at[d], device((x - k + NX) % NX, y, z, core)).start()

    def rx_wait(d):
        return remote(halves.at[d, pl.ds(0, 3)], sides.at[d], rx_send.at[d], rx_recv.at[d], sibling)

    def finish(d):
        rx_wait(d).wait_recv()
        final[d, :, x_lo] = (halves[d, 3].astype(f32) + sides[d, 1].astype(f32)).astype(bf16)
        final[d, :, 1 - x_lo] = (sides[d, 0].astype(f32) + sides[d, 2].astype(f32)).astype(bf16)
        for k in (4, 3, 5, 2, 6, 1, 7, 0):
            if (k, d) == (0, 0):
                local(final.at[d, z], back.at[y, z], own_sem.at[1 + NY]).start()
            else:
                to_z, to_y = (z + k) % NZ, (y - d + NY) % NY
                remote(final.at[d, to_z], back.at[y, z], rz_send, rz_recv.at[d], device(x, to_y, to_z, core)).start()

    def pick(d):
        count, from_y = NZ if d else NZ - 1, (y + d) % NY
        part = back.at[from_y, pl.ds(0, count)]
        remote(part, part, rz_send, rz_recv.at[d], sibling).wait_recv()
        if d == 0:
            local(final.at[d, z], back.at[y, z], own_sem.at[1 + NY]).wait()
        place = lax.broadcasted_iota(jnp.int32, (tokens, 2 * block), 1) + from_y * (2 * block)
        got = back[from_y].reshape(2 * block, features)
        total = None
        for choice in range(TOP):
            mine = jnp.where(place == back_ref[:, choice:choice + 1], 1.0, 0.0).astype(bf16)
            part = gate_ref[:, choice:choice + 1] * jnp.dot(mine, got, preferred_element_type=f32)
            total = part if total is None else total + part
        return total

    spread(0)
    spread(1)
    share(0)
    compute(0)
    spread(3)
    share(1)
    compute(1)
    halve(0)
    spread(2)
    share(3)
    compute(3)
    halve(1)
    finish(0)
    share(2)
    compute(2)
    halve(3)
    finish(1)
    halve(2)
    finish(3)
    finish(2)
    total = pick(0) + pick(1)
    total = total + pick(3)
    total = total + pick(2)
    mix_ref[0] = total.astype(bf16)

    for d in range(NY):
        x_wait(d).wait_send()
        s_wait(d).wait_send()
        rs_wait(d).wait_send()
        rx_wait(d).wait_send()
    for sent_ref, sem in ((came, zy_send), (final, rz_send)):
        some = sent_ref.at[pl.ds(0, NY - 1)]
        remote(some, some, sem, zy_recv.at[0], sibling).wait_send()
        rest = sent_ref.at[0, pl.ds(0, NZ - 1)]
        remote(rest, rest, sem, zy_recv.at[0], sibling).wait_send()
    for chunk in range(len(CHUNKS)):
        z_wait(chunk).wait_send()
        y_wait(chunk).wait_send()
        gx_wait(chunk).wait_send()
        gs_wait(chunk).wait_send()
    kv_wait().wait_send()


def body(
    tokens, expert_ids, attn_gain, w_query, w_kv, w_out, moe_gain, router, w_gate, w_up, w_down
):
    _, rows, features = tokens.shape
    width = w_gate.shape[2]
    heads = w_query.shape[1] // HD
    block = (NZ, CAP, features)
    dma, vmem = pltpu.SemaphoreType.DMA, pltpu.VMEM
    n = len(CHUNKS)
    any_spec, vmem_spec = pl.BlockSpec(memory_space=pl.ANY), pl.BlockSpec(memory_space=vmem)
    return pl.pallas_call(
        layer_kernel,
        out_shape=[jax.ShapeDtypeStruct(tokens.shape, bf16)] * 2,
        in_specs=[vmem_spec] * 5 + [any_spec] * 6,
        out_specs=[vmem_spec] * 2,
        scratch_shapes=[vmem((2, NZ, NY) + w.shape, bf16) for w in (w_query, w_kv, w_out)]
        + [
            vmem((rows, features), bf16),
            vmem((heads, rows, HD), bf16),
            vmem((4, rows, 2 * HD), bf16),
            vmem((rows, heads * HD), bf16),
            vmem((rows, features), bf16),
            vmem((2 * NZ * NY * CAP, rows), bf16),
            vmem((rows, TOP), jnp.int32),
            vmem((rows, TOP), f32),
            vmem((features, width), bf16),
            vmem((features, width), bf16),
            vmem((width, features), bf16),
            vmem((NZ, NY, 2, CAP, features), bf16),
            vmem((NY, NZ, 2, CAP, features), bf16),
            vmem((NY, 2, NX) + block, bf16),
            vmem((2 * NX * NZ * CAP, width), bf16),
            vmem((NY, 2, NX) + block, bf16),
            vmem((NY, NX) + block, bf16),
            vmem((NY, NX) + block, bf16),
            vmem((NY, NX - 1) + block, bf16),
            vmem((NY, NZ, 2, CAP, features), bf16),
            vmem((NY, NZ, 2, CAP, features), bf16),
        ]
        + [dma((n,))] * 9
        + [dma, dma]
        + [
            dma((3,)), dma, dma((NY,)), dma((NY,)), dma((NY,)), dma((NY,)), dma((NY,)), dma((2 + NY,)),
            dma((NY,)), dma((NY,)), dma((NY,)), dma((NY,)), dma, dma((NY,)),
        ],
        compiler_params=pltpu.CompilerParams(collective_id=0, has_side_effects=True, vmem_limit_bytes=60 << 20),
        name="layer",
    )(tokens, expert_ids, attn_gain.reshape(1, -1), moe_gain.reshape(1, -1), router, w_query, w_kv, w_out, w_gate, w_up, w_down)


def solution(mesh):
    in_specs = (
        P("exp", "ctx", None),
        P("exp", "ctx", None),
        P(),
        P("exp", None),
        P("exp", None),
        P("exp", None),
        P(),
        P(),
        P("exp", None, "ctx"),
        P("exp", None, "ctx"),
        P("exp", "ctx", None),
    )
    out_specs = (P("exp", "ctx", None), P("exp", "ctx", None))
    return jax.shard_map(body, mesh=mesh, in_specs=in_specs, out_specs=out_specs, check_vma=False)
```

```python
import functools

import jax
import jax.numpy as jnp
from jax import lax
from jax.experimental import pallas as pl
from jax.experimental.pallas import tpu as pltpu
from jax.sharding import PartitionSpec as P

HD = 128
TOP = 2
MESH = pl.DeviceIdType.MESH
NX, NY, NZ = 4, 4, 8


epsilon = 1e-06
bf16, f32 = jnp.bfloat16, jnp.float32


def rms_scaled(values):
    return values * lax.rsqrt(jnp.mean(values * values, axis=-1, keepdims=True) + epsilon)


def here():
    ctx, exp = lax.axis_index("ctx"), lax.axis_index("exp")
    core, y = ctx % 2, exp % NY
    z, x_lo = (exp // NY) % NZ, exp // (NY * NZ)
    return (ctx // 2) * 2 + x_lo, y, z, core


def device(x, y, z, core):
    return (x // 2) * 2 + core, ((x % 2) * NZ + z) * NY + y


def signal(sem, target):
    pl.semaphore_signal(sem, inc=1, device_id=target, device_id_type=MESH)


CHUNKS = ((1, 0, 128), (0, 0, 256), (0, 256, 256), (2, 0, 256), (2, 256, 256))
TILE = 256
CAP = 6
Q, W = 4, 256
DRAIN = 256


def remote(src, dst, send, recv, target):
    return pltpu.make_async_remote_copy(src_ref=src, dst_ref=dst, send_sem=send, recv_sem=recv, device_id=target, device_id_type=MESH)


def local(src, dst, sem):
    return pltpu.make_async_copy(src, dst, sem)


def layer_kernel(tok_ref, id_ref, again_ref, mgain_ref, router_ref, q_in, kv_in, o_in, wg_hbm, wu_hbm, wd_hbm, att_ref, mix_ref,
                 q_all, kv_all, o_all, normed, queries, key_values, context, moe_ref, quarters, chosen_ref, back_ref, gate_ref, into, outof, many, outcome, mix,
                 wg, wu, wd, sent, came, rows, hidden, terms, theirs, halves, sides, final, back,
                 g_own, z_send, z_recv, y_send, y_recv, gx_send, gx_recv, gs_send, gs_recv, kv_send, kv_recv,
                 w_sem, zy_send, zy_recv, x_send, x_recv, s_send, s_recv, own_sem,
                 rs_send, rs_recv, rx_send, rx_recv, rz_send, rz_recv):
    x, y, z, core = here()
    x_lo = x % 2
    features = tok_ref.shape[2]
    tokens = tok_ref.shape[1]
    experts = router_ref.shape[0]
    block = NZ * CAP
    high = Q * CAP
    plane = [(k, d) for d in (0, 1, 3, 2) for k in (4, 3, 5, 2, 6, 1, 7, 0) if (k, d) != (0, 0)]
    sibling = device(x, y, z, 1 - core)
    barrier = pltpu.get_barrier_semaphore()
    partners = [device(x, (y + d) % NY, (z + k) % NZ, core) for k, d in plane]
    partners += [device((x + k) % NX, y, z, core) for k in range(1, NX)]
    partners += [sibling, device((x + 2) % NX, y, z, 1 - core)]
    for partner in partners:
        signal(barrier, partner)

    ins, outs = (q_in, kv_in, o_in), (q_all, kv_all, o_all)

    def cols(chunk):
        array, first, width = CHUNKS[chunk]
        half = ins[array].shape[1] // 2
        return array, pl.ds(pl.multiple_of(core * half + first, 128), width)

    own = []
    for chunk in range(len(CHUNKS)):
        array, where = cols(chunk)
        copy = local(ins[array].at[:, where], outs[array].at[x_lo, z, y, :, where], g_own.at[chunk])
        copy.start()
        own.append(copy)
    pl.semaphore_wait(barrier, len(partners))
    for chunk in range(len(CHUNKS)):
        array, where = cols(chunk)
        for k in (4, 3, 5, 2, 6, 1, 7):
            remote(ins[array].at[:, where], outs[array].at[x_lo, z, y, :, where], z_send.at[chunk], z_recv.at[chunk],
                   device(x, y, (z + k) % NZ, core)).start()

    def z_wait(chunk):
        array, where = cols(chunk)
        seven = outs[array].at[x_lo, pl.ds(0, NZ - 1), y, :, where]
        return remote(seven, seven, z_send.at[chunk], z_recv.at[chunk], sibling)

    def y_step(chunk):
        array, where = cols(chunk)
        z_wait(chunk).wait_recv()
        own[chunk].wait()
        part = outs[array].at[x_lo, :, y, :, where]
        for k in (2, 1, 3):
            remote(part, part, y_send.at[chunk], y_recv.at[chunk], device(x, (y + k) % NY, z, core)).start()

    def y_wait(chunk):
        array, where = cols(chunk)
        three = outs[array].at[x_lo, :, pl.ds(0, NY - 1), :, where]
        return remote(three, three, y_send.at[chunk], y_recv.at[chunk], sibling)

    def x_step(chunk):
        array, where = cols(chunk)
        y_wait(chunk).wait_recv()
        for k, first in ((1, 0), (3, NZ // 2)):
            part = outs[array].at[x_lo, pl.ds(first, NZ // 2), :, :, where]
            remote(part, part, gx_send.at[chunk], gx_recv.at[chunk], device((x + k) % NX, y, z, core)).start()
        part = outs[array].at[x_lo, :, :, :, where]
        remote(part, part, gs_send.at[chunk], gs_recv.at[chunk], sibling).start()

    def gx_wait(chunk):
        array, where = cols(chunk)
        mine, other = outs[array].at[x_lo, :, :, :, where], outs[array].at[1 - x_lo, :, :, :, where]
        return remote(mine, other, gx_send.at[chunk], gx_recv.at[chunk], sibling)

    def gs_step(chunk):
        array, where = cols(chunk)
        gx_wait(chunk).wait_recv()
        part = outs[array].at[1 - x_lo, :, :, :, where]
        remote(part, part, gs_send.at[chunk], gs_recv.at[chunk], sibling).start()

    def gs_wait(chunk):
        array, first, width = CHUNKS[chunk]
        half = ins[array].shape[1] // 2
        theirs_at = pl.ds(pl.multiple_of((1 - core) * half + first, 128), width)
        _, where = cols(chunk)
        return remote(outs[array].at[:, :, :, :, where], outs[array].at[:, :, :, :, theirs_at], gs_send.at[chunk], gs_recv.at[chunk], sibling)

    floats = tok_ref[0].astype(f32)
    normed[...] = (rms_scaled(floats) * again_ref[...]).astype(bf16)
    lane = lax.broadcasted_iota(jnp.int32, (tokens, experts), 1)
    down, across = (lax.broadcasted_iota(jnp.int32, (tokens, tokens), i) for i in (0, 1))
    ids = [jnp.sum(jnp.where(across == down, id_ref[0, choice:choice + 1, :].astype(f32), 0.0), axis=1, keepdims=True).astype(jnp.int32) for choice in range(TOP)]
    named = [ids[choice] == lane for choice in range(TOP)]
    either = jnp.where(named[0] | named[1], 1.0, 0.0).astype(bf16)
    before = jnp.dot(jnp.where(across < down, 1.0, 0.0).astype(bf16), either, preferred_element_type=f32)
    sent_at = []
    for choice in range(TOP):
        slot = jnp.sum(jnp.where(named[choice], before, 0.0), axis=1, keepdims=True).astype(jnp.int32)
        chip, low = ids[choice] % (NZ * NY), ids[choice] // (NZ * NY)
        back_ref[:, choice:choice + 1] = (((chip % NY) * NZ + chip // NY) * 2 + low) * high + slot
        place = ((chip * 2 + low) * high + slot).astype(f32)
        place = jnp.sum(jnp.where(across == down, place, 0.0), axis=0, keepdims=True).astype(jnp.int32)
        sent_at.append(jnp.concatenate([place + q * CAP for q in range(Q)], axis=1))
    row = lax.broadcasted_iota(jnp.int32, (2 * NZ * NY * high, Q * tokens), 0)
    chosen_ref[...] = jnp.where((row == sent_at[0]) | (row == sent_at[1]), 1.0, 0.0).astype(bf16)
    for ref, a, b in ((into, 0, 1), (outof, 1, 0)):
        to, at = (lax.broadcasted_iota(jnp.int32, (NZ * high, NZ * high), i) for i in (a, b))
        same = (to // block == (at % high) // CAP) & ((to % block) // CAP == at // high) & (to % CAP == at % CAP)
        ref[...] = jnp.where(same, 1.0, 0.0).astype(bf16)
    loads = [local(src.at[0], dst, w_sem.at[i]) for i, (src, dst) in enumerate(((wg_hbm, wg), (wu_hbm, wu), (wd_hbm, wd)))]

    def matrix(ref, tile):
        return ref[:, :, :, :, tile * TILE:(tile + 1) * TILE].reshape(-1, TILE)

    ctx = (x // 2) * 2 + core
    peers = [device((x + 2) % NX, y, z, core), sibling, device((x + 2) % NX, y, z, 1 - core)]

    def make_keys():
        pair = jnp.dot(normed[...], matrix(kv_all, 0), preferred_element_type=f32)
        key_values[ctx, :, :HD] = rms_scaled(pair[:, :HD]).astype(bf16)
        key_values[ctx, :, HD:] = pair[:, HD:].astype(bf16)
        for peer in peers:
            remote(key_values.at[ctx], key_values.at[ctx], kv_send, kv_recv, peer).start()

    def kv_wait():
        three = key_values.at[pl.ds(0, 3)]
        return remote(three, three, kv_send, kv_recv, sibling)

    def make_queries(tile):
        wide = jnp.dot(normed[...], matrix(q_all, tile), preferred_element_type=f32)
        for head in range(TILE // HD):
            queries[tile * 2 + head] = rms_scaled(wide[:, head * HD:(head + 1) * HD]).astype(bf16)

    def attend(tile):
        keys = key_values[:, :, :HD].reshape(-1, HD)
        values = key_values[:, :, HD:].reshape(-1, HD)
        for head in (tile * 2, tile * 2 + 1):
            scores = lax.dot_general(queries[head], keys, (((1,), (1,)), ((), ())), preferred_element_type=f32) * (HD ** (-0.5))
            weights = jnp.exp(scores).astype(bf16)
            weighted = jnp.dot(weights, values, preferred_element_type=f32)
            totals = jnp.sum(weights.astype(f32), axis=1, keepdims=True)
            context[:, head * HD:(head + 1) * HD] = (weighted / totals).astype(bf16)

    def project(tile):
        att_ref[0, :, tile * TILE:(tile + 1) * TILE] = jnp.dot(context[...], matrix(o_all, tile), preferred_element_type=f32).astype(bf16)

    y_step(0)
    y_step(1)
    x_step(0)
    y_step(2)
    x_step(1)
    gs_step(0)
    gs_wait(0).wait_recv()
    make_keys()
    y_step(3)
    x_step(2)
    gs_step(1)
    gs_wait(1).wait_recv()
    make_queries(0)
    make_queries(2)
    y_step(4)
    x_step(3)
    gs_step(2)
    gs_wait(2).wait_recv()
    make_queries(1)
    make_queries(3)
    kv_wait().wait_recv()
    attend(0)
    x_step(4)
    attend(1)
    gs_step(3)
    attend(2)
    attend(3)
    gs_step(4)
    for load in loads:
        load.start()
    gs_wait(3).wait_recv()
    project(0)
    project(2)
    gs_wait(4).wait_recv()
    project(1)
    project(3)
    mixed = floats + att_ref[0].astype(f32)
    moe_ref[...] = (rms_scaled(mixed) * mgain_ref[...]).astype(bf16)

    for q in range(Q):
        quarters[q] = moe_ref[:, q * W:(q + 1) * W]
    sent[...] = jnp.dot(chosen_ref[...], quarters[...].reshape(Q * tokens, W), preferred_element_type=f32).astype(bf16).reshape(sent.shape)
    for k, d in plane:
        to_z, to_y = (z + k) % NZ, (y + d) % NY
        remote(sent.at[to_z, to_y], came.at[d, z], zy_send, zy_recv.at[d], device(x, to_y, to_z, core)).start()
    own_block = local(sent.at[z, y], came.at[0, z], own_sem.at[0])
    own_block.start()
    logits = lax.dot_general(moe_ref[...], router_ref[...], (((1,), (1,)), ((), ())), preferred_element_type=f32)
    picked = [jnp.sum(jnp.where(named[choice], logits, 0.0), axis=1, keepdims=True) for choice in range(TOP)]
    first = jax.nn.sigmoid(picked[0] - picked[1])
    gate_ref[:, 0:1] = first
    gate_ref[:, 1:2] = 1.0 - first

    def zy_wait(d):
        count = NZ if d else NZ - 1
        return remote(came.at[d, pl.ds(0, count)], came.at[d, pl.ds(0, count)], zy_send, zy_recv.at[d], sibling)

    def spread(d):
        zy_wait(d).wait_recv()
        if d == 0:
            own_block.wait()
        for k, part in ((2, x_lo), (1, 1 - x_lo), (3, 1 - x_lo)):
            remote(came.at[d, :, part], rows.at[d, core, k - 1], x_send.at[d], x_recv.at[d], device((x + k) % NX, y, z, core)).start()
        local(came.at[d, :, x_lo], rows.at[d, core, 3], own_sem.at[1 + d]).start()
        remote(came.at[d, :, x_lo], rows.at[d, core, 3], s_send.at[d], s_recv.at[d], sibling).start()

    def x_wait(d):
        three = rows.at[d, core, pl.ds(0, 3)]
        return remote(three, three, x_send.at[d], x_recv.at[d], sibling)

    def share(d):
        x_wait(d).wait_recv()
        three = rows.at[d, core, pl.ds(0, 3)]
        remote(three, three, s_send.at[d], s_recv.at[d], sibling).start()

    def s_wait(d):
        return remote(rows.at[d, core], rows.at[d, 1 - core], s_send.at[d], s_recv.at[d], sibling)

    def compute(d):
        s_wait(d).wait_recv()
        local(came.at[d, :, x_lo], rows.at[d, core, 3], own_sem.at[1 + d]).wait()
        if d == 0:
            for load in loads:
                load.wait()
        for group in range(2 * NX):
            turned = jnp.dot(into[...], rows[d, group // NX, group % NX].reshape(NZ * high, W), preferred_element_type=f32).astype(bf16)
            for q in range(Q):
                many[group * block:(group + 1) * block, q * W:(q + 1) * W] = turned[q * block:(q + 1) * block]

        def up(tile, carry):
            where = pl.ds(pl.multiple_of(tile * DRAIN, DRAIN), DRAIN)
            gated = jnp.dot(many[...], wg[:, where], preferred_element_type=f32)
            lifted = jnp.dot(many[...], wu[:, where], preferred_element_type=f32)
            hidden[:, where] = (gated / (1.0 + jnp.exp(-gated)) * lifted).astype(bf16)
            return carry

        lax.fori_loop(0, wg.shape[1] // DRAIN, up, 0)
        inner = hidden[...]

        def fall(tile, carry):
            where = pl.ds(pl.multiple_of(tile * DRAIN, DRAIN), DRAIN)
            outcome[:, where] = jnp.dot(inner, wd[:, where], preferred_element_type=f32).astype(bf16)
            return carry

        lax.fori_loop(0, features // DRAIN, fall, 0)
        for group in range(2 * NX):
            flat = jnp.concatenate([outcome[group * block:(group + 1) * block, q * W:(q + 1) * W] for q in range(Q)], axis=0)
            turned = jnp.dot(outof[...], flat, preferred_element_type=f32).astype(bf16)
            terms[d, group // NX, group % NX] = turned.reshape(NZ, high, W)
        remote(terms.at[d, 1 - core], theirs.at[d], rs_send.at[d], rs_recv.at[d], sibling).start()

    def rs_wait(d):
        return remote(terms.at[d, 1 - core], theirs.at[d], rs_send.at[d], rs_recv.at[d], sibling)

    def halve(d):
        rs_wait(d).wait_recv()
        halves[d] = (terms[d, core].astype(f32) + theirs[d].astype(f32)).astype(bf16)
        for k in (2, 1, 3):
            remote(halves.at[d, k - 1], sides.at[d, k - 1], rx_send.at[d], rx_recv.at[d], device((x - k + NX) % NX, y, z, core)).start()

    def rx_wait(d):
        return remote(halves.at[d, pl.ds(0, 3)], sides.at[d], rx_send.at[d], rx_recv.at[d], sibling)

    def finish(d):
        rx_wait(d).wait_recv()
        final[d, :, x_lo] = (halves[d, 3].astype(f32) + sides[d, 1].astype(f32)).astype(bf16)
        final[d, :, 1 - x_lo] = (sides[d, 0].astype(f32) + sides[d, 2].astype(f32)).astype(bf16)
        for k in (4, 3, 5, 2, 6, 1, 7, 0):
            if (k, d) == (0, 0):
                local(final.at[d, z], back.at[y, z], own_sem.at[1 + NY]).start()
            else:
                to_z, to_y = (z + k) % NZ, (y - d + NY) % NY
                remote(final.at[d, to_z], back.at[y, z], rz_send, rz_recv.at[d], device(x, to_y, to_z, core)).start()

    def pick(d, first_pick=False):
        count, from_y = NZ if d else NZ - 1, (y + d) % NY
        part = back.at[from_y, pl.ds(0, count)]
        remote(part, part, rz_send, rz_recv.at[d], sibling).wait_recv()
        if d == 0:
            local(final.at[d, z], back.at[y, z], own_sem.at[1 + NY]).wait()
        place = lax.broadcasted_iota(jnp.int32, (tokens, 2 * NZ * high), 1) + from_y * (2 * NZ * high)
        got = back[from_y].reshape(2 * NZ * high, W)
        for q in range(Q):
            total = None
            for choice in range(TOP):
                mine = jnp.where(place == back_ref[:, choice:choice + 1] + q * CAP, 1.0, 0.0).astype(bf16)
                part = gate_ref[:, choice:choice + 1] * jnp.dot(mine, got, preferred_element_type=f32)
                total = part if total is None else total + part
            if first_pick:
                mix[:, q * W:(q + 1) * W] = total
            else:
                mix[:, q * W:(q + 1) * W] += total

    spread(0)
    spread(1)
    share(0)
    compute(0)
    spread(3)
    share(1)
    compute(1)
    halve(0)
    spread(2)
    share(3)
    compute(3)
    halve(1)
    finish(0)
    share(2)
    compute(2)
    halve(3)
    finish(1)
    pick(0, True)
    halve(2)
    finish(3)
    pick(1)
    finish(2)
    pick(3)
    pick(2)
    mix_ref[0] = mix[...].astype(bf16)

    for d in range(NY):
        x_wait(d).wait_send()
        s_wait(d).wait_send()
        rs_wait(d).wait_send()
        rx_wait(d).wait_send()
    for sent_ref, sem in ((came, zy_send), (final, rz_send)):
        some = sent_ref.at[pl.ds(0, NY - 1)]
        remote(some, some, sem, zy_recv.at[0], sibling).wait_send()
        rest = sent_ref.at[0, pl.ds(0, NZ - 1)]
        remote(rest, rest, sem, zy_recv.at[0], sibling).wait_send()
    for chunk in range(len(CHUNKS)):
        z_wait(chunk).wait_send()
        y_wait(chunk).wait_send()
        gx_wait(chunk).wait_send()
        gs_wait(chunk).wait_send()
    kv_wait().wait_send()


def settle(a_ref, b_ref, a_out, b_out, sem):
    copies = [local(a_ref, a_out, sem.at[0]), local(b_ref, b_out, sem.at[1])]
    for copy in copies:
        copy.start()
    for copy in copies:
        copy.wait()


def body(
    tokens, expert_ids, attn_gain, w_query, w_kv, w_out, moe_gain, router, w_gate, w_up, w_down
):
    _, rows, features = tokens.shape
    width = w_gate.shape[2]
    heads = w_query.shape[1] // HD
    block = (NZ, Q * CAP, W)
    piece = (2, Q * CAP, W)
    dma, vmem = pltpu.SemaphoreType.DMA, pltpu.VMEM
    n = len(CHUNKS)
    any_spec, vmem_spec = pl.BlockSpec(memory_space=pl.ANY), pl.BlockSpec(memory_space=vmem)
    results = pl.pallas_call(
        layer_kernel,
        out_shape=[jax.ShapeDtypeStruct(tokens.shape, bf16)] * 2,
        in_specs=[vmem_spec] * 5 + [any_spec] * 6,
        out_specs=[vmem_spec] * 2,
        scratch_shapes=[vmem((2, NZ, NY) + w.shape, bf16) for w in (w_query, w_kv, w_out)]
        + [
            vmem((rows, features), bf16),
            vmem((heads, rows, HD), bf16),
            vmem((4, rows, 2 * HD), bf16),
            vmem((rows, heads * HD), bf16),
            vmem((rows, features), bf16),
            vmem((Q, rows, W), bf16),
            vmem((2 * NZ * NY * Q * CAP, Q * rows), bf16),
            vmem((rows, TOP), jnp.int32),
            vmem((rows, TOP), f32),
            vmem((NZ * Q * CAP, NZ * Q * CAP), bf16),
            vmem((NZ * Q * CAP, NZ * Q * CAP), bf16),
            vmem((2 * NX * NZ * CAP, features), bf16),
            vmem((2 * NX * NZ * CAP, features), bf16),
            vmem((rows, features), f32),
            vmem((features, width), bf16),
            vmem((features, width), bf16),
            vmem((width, features), bf16),
            vmem((NZ, NY) + piece, bf16),
            vmem((NY, NZ) + piece, bf16),
            vmem((NY, 2, NX) + block, bf16),
            vmem((2 * NX * NZ * CAP, width), bf16),
            vmem((NY, 2, NX) + block, bf16),
            vmem((NY, NX) + block, bf16),
            vmem((NY, NX) + block, bf16),
            vmem((NY, NX - 1) + block, bf16),
            vmem((NY, NZ) + piece, bf16),
            vmem((NY, NZ) + piece, bf16),
        ]
        + [dma((n,))] * 9
        + [dma, dma]
        + [
            dma((3,)), dma, dma((NY,)), dma((NY,)), dma((NY,)), dma((NY,)), dma((NY,)), dma((2 + NY,)),
            dma((NY,)), dma((NY,)), dma((NY,)), dma((NY,)), dma, dma((NY,)),
        ],
        compiler_params=pltpu.CompilerParams(collective_id=0, has_side_effects=True, vmem_limit_bytes=60 << 20),
        name="layer",
    )(tokens, expert_ids.swapaxes(1, 2), attn_gain.reshape(1, -1), moe_gain.reshape(1, -1), router.T, w_query, w_kv, w_out, w_gate, w_up, w_down)
    return tuple(pl.pallas_call(
        settle,
        out_shape=[jax.ShapeDtypeStruct(tokens.shape, bf16)] * 2,
        in_specs=[any_spec] * 2,
        out_specs=[any_spec] * 2,
        scratch_shapes=[dma((2,))],
        name="settle",
    )(*results))


def solution(mesh):
    in_specs = (
        P("exp", "ctx", None),
        P("exp", "ctx", None),
        P(),
        P("exp", None),
        P("exp", None),
        P("exp", None),
        P(),
        P(),
        P("exp", None, "ctx"),
        P("exp", None, "ctx"),
        P("exp", "ctx", None),
    )
    out_specs = (P("exp", "ctx", None), P("exp", "ctx", None))
    return jax.shard_map(body, mesh=mesh, in_specs=in_specs, out_specs=out_specs, check_vma=False)
```

```python
import functools

import jax
import jax.numpy as jnp
from jax import lax
from jax.experimental import pallas as pl
from jax.experimental.pallas import tpu as pltpu
from jax.sharding import PartitionSpec as P

HD = 128
TOP = 2
MESH = pl.DeviceIdType.MESH
NX, NY, NZ = 4, 4, 8


epsilon = 1e-06
bf16, f32 = jnp.bfloat16, jnp.float32


def rms_scaled(values):
    return values * lax.rsqrt(jnp.mean(values * values, axis=-1, keepdims=True) + epsilon)


def here():
    ctx, exp = lax.axis_index("ctx"), lax.axis_index("exp")
    core, y = ctx % 2, exp % NY
    z, x_lo = (exp // NY) % NZ, exp // (NY * NZ)
    return (ctx // 2) * 2 + x_lo, y, z, core


def device(x, y, z, core):
    return (x // 2) * 2 + core, ((x % 2) * NZ + z) * NY + y


def signal(sem, target):
    pl.semaphore_signal(sem, inc=1, device_id=target, device_id_type=MESH)


CHUNKS = ((1, 0, 128), (0, 0, 256), (0, 256, 256), (2, 0, 256), (2, 256, 256))
TILE = 256
CAP = 6
Q, W = 4, 256


def remote(src, dst, send, recv, target):
    return pltpu.make_async_remote_copy(src_ref=src, dst_ref=dst, send_sem=send, recv_sem=recv, device_id=target, device_id_type=MESH)


def local(src, dst, sem):
    return pltpu.make_async_copy(src, dst, sem)


def layer_kernel(tok_ref, id_ref, again_ref, mgain_ref, router_ref, q_in, kv_in, o_in, wg_hbm, wu_hbm, wd_hbm, att_ref, mix_ref,
                 q_all, kv_all, o_all, normed, queries, key_values, context, moe_ref, quarters, chosen_ref, back_ref, gate_ref, into, outof, many, outcome, mix,
                 wg, wu, wd, sent, came, rows, hidden, terms, theirs, halves, sides, final, back,
                 g_own, z_send, z_recv, y_send, y_recv, gx_send, gx_recv, gs_send, gs_recv, kv_send, kv_recv,
                 w_sem, zy_send, zy_recv, x_send, x_recv, s_send, s_recv, own_sem,
                 rs_send, rs_recv, rx_send, rx_recv, rz_send, rz_recv):
    x, y, z, core = here()
    x_lo = x % 2
    features = tok_ref.shape[2]
    tokens = tok_ref.shape[1]
    experts = router_ref.shape[0]
    block = NZ * CAP
    high = Q * CAP
    sibling = device(x, y, z, 1 - core)
    barrier = pltpu.get_barrier_semaphore()
    partners = [device(x, y, (z + k) % NZ, core) for k in range(1, NZ)] + [device(x, (y + k) % NY, z, core) for k in range(1, NY)]
    partners += [device((x + k) % NX, y, z, core) for k in range(1, NX)]
    partners += [sibling, device((x + 2) % NX, y, z, 1 - core)]
    for partner in partners:
        signal(barrier, partner)

    ins, outs = (q_in, kv_in, o_in), (q_all, kv_all, o_all)

    def cols(chunk):
        array, first, width = CHUNKS[chunk]
        half = ins[array].shape[1] // 2
        return array, pl.ds(pl.multiple_of(core * half + first, 128), width)

    def span(array):
        half = ins[array].shape[1] // 2
        return pl.ds(pl.multiple_of(core * half, 128), half)

    own = {}
    for array in (1, 0, 2):
        own[array] = local(ins[array].at[:, span(array)], outs[array].at[x_lo, z, y, :, span(array)], g_own.at[array])
        own[array].start()
    pl.semaphore_wait(barrier, len(partners))
    for array in (1, 0, 2):
        for k in (4, 3, 5, 2, 6, 1, 7):
            remote(ins[array].at[:, span(array)], outs[array].at[x_lo, z, y, :, span(array)], z_send.at[array], z_recv.at[array],
                   device(x, y, (z + k) % NZ, core)).start()

    def z_wait(array):
        seven = outs[array].at[x_lo, pl.ds(0, NZ - 1), y, :, span(array)]
        return remote(seven, seven, z_send.at[array], z_recv.at[array], sibling)

    def y_step(chunk):
        array, where = cols(chunk)
        if CHUNKS[chunk][1] == 0:
            z_wait(array).wait_recv()
            own[array].wait()
        part = outs[array].at[x_lo, :, y, :, where]
        for k in (2, 1, 3):
            remote(part, part, y_send.at[chunk], y_recv.at[chunk], device(x, (y + k) % NY, z, core)).start()

    def y_wait(chunk):
        array, where = cols(chunk)
        three = outs[array].at[x_lo, :, pl.ds(0, NY - 1), :, where]
        return remote(three, three, y_send.at[chunk], y_recv.at[chunk], sibling)

    def x_step(chunk):
        array, where = cols(chunk)
        y_wait(chunk).wait_recv()
        for k, first in ((1, 0), (3, NZ // 2)):
            part = outs[array].at[x_lo, pl.ds(first, NZ // 2), :, :, where]
            remote(part, part, gx_send.at[chunk], gx_recv.at[chunk], device((x + k) % NX, y, z, core)).start()
        part = outs[array].at[x_lo, :, :, :, where]
        remote(part, part, gs_send.at[chunk], gs_recv.at[chunk], sibling).start()

    def gx_wait(chunk):
        array, where = cols(chunk)
        mine, other = outs[array].at[x_lo, :, :, :, where], outs[array].at[1 - x_lo, :, :, :, where]
        return remote(mine, other, gx_send.at[chunk], gx_recv.at[chunk], sibling)

    def gs_step(chunk):
        array, where = cols(chunk)
        gx_wait(chunk).wait_recv()
        part = outs[array].at[1 - x_lo, :, :, :, where]
        remote(part, part, gs_send.at[chunk], gs_recv.at[chunk], sibling).start()

    def gs_wait(chunk):
        array, first, width = CHUNKS[chunk]
        half = ins[array].shape[1] // 2
        theirs_at = pl.ds(pl.multiple_of((1 - core) * half + first, 128), width)
        _, where = cols(chunk)
        return remote(outs[array].at[:, :, :, :, where], outs[array].at[:, :, :, :, theirs_at], gs_send.at[chunk], gs_recv.at[chunk], sibling)

    floats = tok_ref[0].astype(f32)
    normed[...] = (rms_scaled(floats) * again_ref[...]).astype(bf16)
    loads = [local(src.at[0], dst, w_sem.at[i]) for i, (src, dst) in enumerate(((wg_hbm, wg), (wu_hbm, wu), (wd_hbm, wd)))]

    def matrix(ref, tile):
        return ref[:, :, :, :, tile * TILE:(tile + 1) * TILE].reshape(-1, TILE)

    ctx = (x // 2) * 2 + core
    peers = [device((x + 2) % NX, y, z, core), sibling, device((x + 2) % NX, y, z, 1 - core)]

    def make_keys():
        pair = jnp.dot(normed[...], matrix(kv_all, 0), preferred_element_type=f32)
        key_values[ctx, :, :HD] = rms_scaled(pair[:, :HD]).astype(bf16)
        key_values[ctx, :, HD:] = pair[:, HD:].astype(bf16)
        for peer in peers:
            remote(key_values.at[ctx], key_values.at[ctx], kv_send, kv_recv, peer).start()

    def kv_wait():
        three = key_values.at[pl.ds(0, 3)]
        return remote(three, three, kv_send, kv_recv, sibling)

    def make_queries(tile):
        wide = jnp.dot(normed[...], matrix(q_all, tile), preferred_element_type=f32)
        for head in range(TILE // HD):
            queries[tile * 2 + head] = rms_scaled(wide[:, head * HD:(head + 1) * HD]).astype(bf16)

    def attend(tile):
        keys = key_values[:, :, :HD].reshape(-1, HD)
        values = key_values[:, :, HD:].reshape(-1, HD)
        for head in (tile * 2, tile * 2 + 1):
            scores = lax.dot_general(queries[head], keys, (((1,), (1,)), ((), ())), preferred_element_type=f32) * (HD ** (-0.5))
            weights = jnp.exp(scores).astype(bf16)
            weighted = jnp.dot(weights, values, preferred_element_type=f32)
            totals = jnp.sum(weights.astype(f32), axis=1, keepdims=True)
            context[:, head * HD:(head + 1) * HD] = (weighted / totals).astype(bf16)

    def project(tile):
        att_ref[0, :, tile * TILE:(tile + 1) * TILE] = jnp.dot(context[...], matrix(o_all, tile), preferred_element_type=f32).astype(bf16)

    y_step(0)
    y_step(1)
    x_step(0)
    y_step(2)
    x_step(1)
    gs_step(0)
    gs_wait(0).wait_recv()
    make_keys()
    y_step(3)
    x_step(2)
    gs_step(1)
    gs_wait(1).wait_recv()
    make_queries(0)
    make_queries(2)
    y_step(4)
    x_step(3)
    lane = lax.broadcasted_iota(jnp.int32, (tokens, experts), 1)
    down, across = (lax.broadcasted_iota(jnp.int32, (tokens, tokens), i) for i in (0, 1))
    ids = [jnp.sum(jnp.where(across == down, id_ref[0, choice:choice + 1, :].astype(f32), 0.0), axis=1, keepdims=True).astype(jnp.int32) for choice in range(TOP)]
    named = [ids[choice] == lane for choice in range(TOP)]
    either = jnp.where(named[0] | named[1], 1.0, 0.0).astype(bf16)
    before = jnp.dot(jnp.where(across < down, 1.0, 0.0).astype(bf16), either, preferred_element_type=f32)
    sent_at = []
    for choice in range(TOP):
        slot = jnp.sum(jnp.where(named[choice], before, 0.0), axis=1, keepdims=True).astype(jnp.int32)
        chip, low = ids[choice] % (NZ * NY), ids[choice] // (NZ * NY)
        place = (((chip % NY) * NZ + chip // NY) * 2 + low) * high + slot
        back_ref[:, choice:choice + 1] = place
        place = jnp.sum(jnp.where(across == down, place.astype(f32), 0.0), axis=0, keepdims=True).astype(jnp.int32)
        sent_at.append(jnp.concatenate([place + q * CAP for q in range(Q)], axis=1))
    row = lax.broadcasted_iota(jnp.int32, (2 * NZ * NY * high, Q * tokens), 0)
    chosen_ref[...] = jnp.where((row == sent_at[0]) | (row == sent_at[1]), 1.0, 0.0).astype(bf16)
    for ref, a, b in ((into, 0, 1), (outof, 1, 0)):
        to, at = (lax.broadcasted_iota(jnp.int32, (NZ * high, NZ * high), i) for i in (a, b))
        same = (to // block == (at % high) // CAP) & ((to % block) // CAP == at // high) & (to % CAP == at % CAP)
        ref[...] = jnp.where(same, 1.0, 0.0).astype(bf16)
    gs_step(2)
    gs_wait(2).wait_recv()
    make_queries(1)
    make_queries(3)
    kv_wait().wait_recv()
    attend(0)
    x_step(4)
    attend(1)
    gs_step(3)
    attend(2)
    attend(3)
    gs_step(4)
    for load in loads:
        load.start()
    gs_wait(3).wait_recv()
    project(0)
    project(2)
    gs_wait(4).wait_recv()
    project(1)
    project(3)
    mixed = floats + att_ref[0].astype(f32)
    moe_ref[...] = (rms_scaled(mixed) * mgain_ref[...]).astype(bf16)

    for q in range(Q):
        quarters[q] = moe_ref[:, q * W:(q + 1) * W]
    for d in (0, 1, 3, 2):
        to_y = (y + d) % NY
        part = chosen_ref[pl.ds(pl.multiple_of(to_y * (2 * NZ * high), 2 * NZ * high), 2 * NZ * high), :]
        sent[to_y] = jnp.dot(part, quarters[...].reshape(Q * tokens, W), preferred_element_type=f32).astype(bf16).reshape(NZ, 2, high, W)
        for k in (4, 3, 5, 2, 6, 1, 7, 0):
            to_z = (z + k) % NZ
            if (k, d) != (0, 0):
                remote(sent.at[to_y, to_z], came.at[d, z], zy_send, zy_recv.at[d], device(x, to_y, to_z, core)).start()
    own_block = local(sent.at[y, z], came.at[0, z], own_sem.at[0])
    own_block.start()
    logits = lax.dot_general(moe_ref[...], router_ref[...], (((1,), (1,)), ((), ())), preferred_element_type=f32)
    picked = [jnp.sum(jnp.where(named[choice], logits, 0.0), axis=1, keepdims=True) for choice in range(TOP)]
    first = jax.nn.sigmoid(picked[0] - picked[1])
    gate_ref[:, 0:1] = first
    gate_ref[:, 1:2] = 1.0 - first

    def zy_wait(d):
        count = NZ if d else NZ - 1
        return remote(came.at[d, pl.ds(0, count)], came.at[d, pl.ds(0, count)], zy_send, zy_recv.at[d], sibling)

    def spread(d):
        zy_wait(d).wait_recv()
        if d == 0:
            own_block.wait()
        for k, part in ((2, x_lo), (1, 1 - x_lo), (3, 1 - x_lo)):
            remote(came.at[d, :, part], rows.at[d, core, k - 1], x_send.at[d], x_recv.at[d], device((x + k) % NX, y, z, core)).start()
        local(came.at[d, :, x_lo], rows.at[d, core, 3], own_sem.at[1 + d]).start()
        remote(came.at[d, :, x_lo], rows.at[d, core, 3], s_send.at[d], s_recv.at[d], sibling).start()

    def x_wait(d):
        three = rows.at[d, core, pl.ds(0, 3)]
        return remote(three, three, x_send.at[d], x_recv.at[d], sibling)

    def share(d):
        x_wait(d).wait_recv()
        three = rows.at[d, core, pl.ds(0, 3)]
        remote(three, three, s_send.at[d], s_recv.at[d], sibling).start()

    def s_wait(d):
        return remote(rows.at[d, core], rows.at[d, 1 - core], s_send.at[d], s_recv.at[d], sibling)

    def compute(d):
        s_wait(d).wait_recv()
        local(came.at[d, :, x_lo], rows.at[d, core, 3], own_sem.at[1 + d]).wait()
        if d == 0:
            for load in loads:
                load.wait()
        for group in range(2 * NX):
            turned = jnp.dot(into[...], rows[d, group // NX, group % NX].reshape(NZ * high, W), preferred_element_type=f32).astype(bf16)
            for q in range(Q):
                many[group * block:(group + 1) * block, q * W:(q + 1) * W] = turned[q * block:(q + 1) * block]

        gated = jnp.dot(many[...], wg[...], preferred_element_type=f32)
        lifted = jnp.dot(many[...], wu[...], preferred_element_type=f32)
        hidden[...] = (gated / (1.0 + jnp.exp(-gated)) * lifted).astype(bf16)
        outcome[...] = jnp.dot(hidden[...], wd[...], preferred_element_type=f32).astype(bf16)
        for group in range(2 * NX):
            flat = jnp.concatenate([outcome[group * block:(group + 1) * block, q * W:(q + 1) * W] for q in range(Q)], axis=0)
            turned = jnp.dot(outof[...], flat, preferred_element_type=f32).astype(bf16)
            terms[d, group // NX, group % NX] = turned.reshape(NZ, high, W)
        remote(terms.at[d, 1 - core], theirs.at[d], rs_send.at[d], rs_recv.at[d], sibling).start()

    def rs_wait(d):
        return remote(terms.at[d, 1 - core], theirs.at[d], rs_send.at[d], rs_recv.at[d], sibling)

    def halve(d):
        rs_wait(d).wait_recv()
        halves[d] = (terms[d, core].astype(f32) + theirs[d].astype(f32)).astype(bf16)
        for k in (2, 1, 3):
            remote(halves.at[d, k - 1], sides.at[d, k - 1], rx_send.at[d], rx_recv.at[d], device((x - k + NX) % NX, y, z, core)).start()

    def rx_wait(d):
        return remote(halves.at[d, pl.ds(0, 3)], sides.at[d], rx_send.at[d], rx_recv.at[d], sibling)

    def finish(d):
        rx_wait(d).wait_recv()
        final[d, :, x_lo] = (halves[d, 3].astype(f32) + sides[d, 1].astype(f32)).astype(bf16)
        final[d, :, 1 - x_lo] = (sides[d, 0].astype(f32) + sides[d, 2].astype(f32)).astype(bf16)
        for k in (4, 3, 5, 2, 6, 1, 7, 0):
            if (k, d) == (0, 0):
                local(final.at[d, z], back.at[y, z], own_sem.at[1 + NY]).start()
            else:
                to_z, to_y = (z + k) % NZ, (y - d + NY) % NY
                remote(final.at[d, to_z], back.at[y, z], rz_send, rz_recv.at[d], device(x, to_y, to_z, core)).start()

    def pick(d, first_pick=False):
        count, from_y = NZ if d else NZ - 1, (y + d) % NY
        part = back.at[from_y, pl.ds(0, count)]
        remote(part, part, rz_send, rz_recv.at[d], sibling).wait_recv()
        if d == 0:
            local(final.at[d, z], back.at[y, z], own_sem.at[1 + NY]).wait()
        place = lax.broadcasted_iota(jnp.int32, (tokens, 2 * NZ * high), 1) + from_y * (2 * NZ * high)
        got = back[from_y].reshape(2 * NZ * high, W)
        for q in range(Q):
            total = None
            for choice in range(TOP):
                mine = jnp.where(place == back_ref[:, choice:choice + 1] + q * CAP, 1.0, 0.0).astype(bf16)
                part = gate_ref[:, choice:choice + 1] * jnp.dot(mine, got, preferred_element_type=f32)
                total = part if total is None else total + part
            if first_pick:
                mix[:, q * W:(q + 1) * W] = total
            else:
                mix[:, q * W:(q + 1) * W] += total

    spread(0)
    spread(1)
    share(0)
    compute(0)
    spread(3)
    share(1)
    compute(1)
    halve(0)
    spread(2)
    share(3)
    compute(3)
    halve(1)
    finish(0)
    share(2)
    compute(2)
    halve(3)
    finish(1)
    pick(0, True)
    halve(2)
    finish(3)
    pick(1)
    finish(2)
    pick(3)
    pick(2)
    mix_ref[0] = mix[...].astype(bf16)

    for d in range(NY):
        x_wait(d).wait_send()
        s_wait(d).wait_send()
        rs_wait(d).wait_send()
        rx_wait(d).wait_send()
    for sent_ref, sem in ((came, zy_send), (final, rz_send)):
        some = sent_ref.at[pl.ds(0, NY - 1)]
        remote(some, some, sem, zy_recv.at[0], sibling).wait_send()
        rest = sent_ref.at[0, pl.ds(0, NZ - 1)]
        remote(rest, rest, sem, zy_recv.at[0], sibling).wait_send()
    for array in range(3):
        z_wait(array).wait_send()
    for chunk in range(len(CHUNKS)):
        y_wait(chunk).wait_send()
        gx_wait(chunk).wait_send()
        gs_wait(chunk).wait_send()
    kv_wait().wait_send()


def settle(a_ref, b_ref, a_out, b_out):
    a_out[...] = a_ref[...]
    b_out[...] = b_ref[...]


def body(
    tokens, expert_ids, attn_gain, w_query, w_kv, w_out, moe_gain, router, w_gate, w_up, w_down
):
    _, rows, features = tokens.shape
    width = w_gate.shape[2]
    heads = w_query.shape[1] // HD
    block = (NZ, Q * CAP, W)
    piece = (2, Q * CAP, W)
    dma, vmem = pltpu.SemaphoreType.DMA, pltpu.VMEM
    n = len(CHUNKS)
    any_spec, vmem_spec = pl.BlockSpec(memory_space=pl.ANY), pl.BlockSpec(memory_space=vmem)
    results = pl.pallas_call(
        layer_kernel,
        out_shape=[jax.ShapeDtypeStruct(tokens.shape, bf16)] * 2,
        in_specs=[vmem_spec] * 5 + [any_spec] * 6,
        out_specs=[vmem_spec] * 2,
        scratch_shapes=[vmem((2, NZ, NY) + w.shape, bf16) for w in (w_query, w_kv, w_out)]
        + [
            vmem((rows, features), bf16),
            vmem((heads, rows, HD), bf16),
            vmem((4, rows, 2 * HD), bf16),
            vmem((rows, heads * HD), bf16),
            vmem((rows, features), bf16),
            vmem((Q, rows, W), bf16),
            vmem((2 * NZ * NY * Q * CAP, Q * rows), bf16),
            vmem((rows, TOP), jnp.int32),
            vmem((rows, TOP), f32),
            vmem((NZ * Q * CAP, NZ * Q * CAP), bf16),
            vmem((NZ * Q * CAP, NZ * Q * CAP), bf16),
            vmem((2 * NX * NZ * CAP, features), bf16),
            vmem((2 * NX * NZ * CAP, features), bf16),
            vmem((rows, features), f32),
            vmem((features, width), bf16),
            vmem((features, width), bf16),
            vmem((width, features), bf16),
            vmem((NY, NZ) + piece, bf16),
            vmem((NY, NZ) + piece, bf16),
            vmem((NY, 2, NX) + block, bf16),
            vmem((2 * NX * NZ * CAP, width), bf16),
            vmem((NY, 2, NX) + block, bf16),
            vmem((NY, NX) + block, bf16),
            vmem((NY, NX) + block, bf16),
            vmem((NY, NX - 1) + block, bf16),
            vmem((NY, NZ) + piece, bf16),
            vmem((NY, NZ) + piece, bf16),
        ]
        + [dma((n,))] * 9
        + [dma, dma]
        + [
            dma((3,)), dma, dma((NY,)), dma((NY,)), dma((NY,)), dma((NY,)), dma((NY,)), dma((2 + NY,)),
            dma((NY,)), dma((NY,)), dma((NY,)), dma((NY,)), dma, dma((NY,)),
        ],
        compiler_params=pltpu.CompilerParams(collective_id=0, has_side_effects=True, vmem_limit_bytes=60 << 20),
        name="layer",
    )(tokens, expert_ids.swapaxes(1, 2), attn_gain.reshape(1, -1), moe_gain.reshape(1, -1), router.T, w_query, w_kv, w_out, w_gate, w_up, w_down)
    return tuple(pl.pallas_call(
        settle,
        out_shape=[jax.ShapeDtypeStruct(tokens.shape, bf16)] * 2,
        in_specs=[vmem_spec] * 2,
        out_specs=[vmem_spec] * 2,
        name="settle",
    )(*results))


def solution(mesh):
    in_specs = (
        P("exp", "ctx", None),
        P("exp", "ctx", None),
        P(),
        P("exp", None),
        P("exp", None),
        P("exp", None),
        P(),
        P(),
        P("exp", None, "ctx"),
        P("exp", None, "ctx"),
        P("exp", "ctx", None),
    )
    out_specs = (P("exp", "ctx", None), P("exp", "ctx", None))
    return jax.shard_map(body, mesh=mesh, in_specs=in_specs, out_specs=out_specs, check_vma=False)
```

```python
import functools

import jax
import jax.numpy as jnp
from jax import lax
from jax.experimental import pallas as pl
from jax.experimental.pallas import tpu as pltpu
from jax.sharding import PartitionSpec as P

HD = 128
TOP = 2
MESH = pl.DeviceIdType.MESH
NX, NY, NZ = 4, 4, 8


epsilon = 1e-06
bf16, f32 = jnp.bfloat16, jnp.float32


def rms_scaled(values):
    return values * lax.rsqrt(jnp.mean(values * values, axis=-1, keepdims=True) + epsilon)


def here():
    ctx, exp = lax.axis_index("ctx"), lax.axis_index("exp")
    core, y = ctx % 2, exp % NY
    z, x_lo = (exp // NY) % NZ, exp // (NY * NZ)
    return (ctx // 2) * 2 + x_lo, y, z, core


def device(x, y, z, core):
    return (x // 2) * 2 + core, ((x % 2) * NZ + z) * NY + y


def signal(sem, target):
    pl.semaphore_signal(sem, inc=1, device_id=target, device_id_type=MESH)


CHUNKS = ((1, 0, 128), (0, 0, 256), (0, 256, 256), (2, 0, 256), (2, 256, 256))
TILE = 256
CAP = 6
Q, W = 4, 256


def remote(src, dst, send, recv, target):
    return pltpu.make_async_remote_copy(src_ref=src, dst_ref=dst, send_sem=send, recv_sem=recv, device_id=target, device_id_type=MESH)


def local(src, dst, sem):
    return pltpu.make_async_copy(src, dst, sem)


def layer_kernel(tok_ref, id_ref, again_ref, mgain_ref, router_ref, q_in, kv_in, o_in, wg_hbm, wu_hbm, wd_hbm, att_ref, mix_ref,
                 q_all, kv_all, o_all, normed, queries, key_values, context, moe_ref, quarters, chosen_ref, back_ref, gate_ref, into, outof, many, outcome, mix,
                 wg, wu, wd, sent, came, rows, hidden, terms, theirs, halves, sides, final, back,
                 g_own, z_send, z_recv, y_send, y_recv, gx_send, gx_recv, gs_send, gs_recv, kv_send, kv_recv,
                 w_sem, zy_send, zy_recv, x_send, x_recv, s_send, s_recv, own_sem,
                 rs_send, rs_recv, rx_send, rx_recv, rz_send, rz_recv):
    x, y, z, core = here()
    x_lo = x % 2
    features = tok_ref.shape[2]
    tokens = tok_ref.shape[1]
    experts = router_ref.shape[0]
    block = NZ * CAP
    high = Q * CAP
    sibling = device(x, y, z, 1 - core)
    barrier = pltpu.get_barrier_semaphore()
    partners = [device(x, y, (z + k) % NZ, core) for k in range(1, NZ)] + [device(x, (y + k) % NY, z, core) for k in range(1, NY)]
    partners += [device((x + k) % NX, y, z, core) for k in range(1, NX)]
    partners += [sibling, device((x + 2) % NX, y, z, 1 - core)]
    for partner in partners:
        signal(barrier, partner)

    ins, outs = (q_in, kv_in, o_in), (q_all, kv_all, o_all)

    def cols(chunk):
        array, first, width = CHUNKS[chunk]
        half = ins[array].shape[1] // 2
        return array, pl.ds(pl.multiple_of(core * half + first, 128), width)

    own = []
    for chunk in range(len(CHUNKS)):
        array, where = cols(chunk)
        copy = local(ins[array].at[:, where], outs[array].at[x_lo, z, y, :, where], g_own.at[chunk])
        copy.start()
        own.append(copy)
    pl.semaphore_wait(barrier, len(partners))
    for chunk in range(len(CHUNKS)):
        array, where = cols(chunk)
        for k in (4, 3, 5, 2, 6, 1, 7):
            remote(ins[array].at[:, where], outs[array].at[x_lo, z, y, :, where], z_send.at[chunk], z_recv.at[chunk],
                   device(x, y, (z + k) % NZ, core)).start()

    def z_wait(chunk):
        array, where = cols(chunk)
        seven = outs[array].at[x_lo, pl.ds(0, NZ - 1), y, :, where]
        return remote(seven, seven, z_send.at[chunk], z_recv.at[chunk], sibling)

    def y_step(chunk):
        array, where = cols(chunk)
        z_wait(chunk).wait_recv()
        own[chunk].wait()
        part = outs[array].at[x_lo, :, y, :, where]
        for k in (2, 1, 3):
            remote(part, part, y_send.at[chunk], y_recv.at[chunk], device(x, (y + k) % NY, z, core)).start()

    def y_wait(chunk):
        array, where = cols(chunk)
        three = outs[array].at[x_lo, :, pl.ds(0, NY - 1), :, where]
        return remote(three, three, y_send.at[chunk], y_recv.at[chunk], sibling)

    def x_step(chunk):
        array, where = cols(chunk)
        y_wait(chunk).wait_recv()
        for k, first in ((1, 0), (3, NZ // 2)):
            part = outs[array].at[x_lo, pl.ds(first, NZ // 2), :, :, where]
            remote(part, part, gx_send.at[chunk], gx_recv.at[chunk], device((x + k) % NX, y, z, core)).start()
        part = outs[array].at[x_lo, :, :, :, where]
        remote(part, part, gs_send.at[chunk], gs_recv.at[chunk], sibling).start()

    def gx_wait(chunk):
        array, where = cols(chunk)
        mine, other = outs[array].at[x_lo, :, :, :, where], outs[array].at[1 - x_lo, :, :, :, where]
        return remote(mine, other, gx_send.at[chunk], gx_recv.at[chunk], sibling)

    def gs_step(chunk):
        array, where = cols(chunk)
        gx_wait(chunk).wait_recv()
        part = outs[array].at[1 - x_lo, :, :, :, where]
        remote(part, part, gs_send.at[chunk], gs_recv.at[chunk], sibling).start()

    def gs_wait(chunk):
        array, first, width = CHUNKS[chunk]
        half = ins[array].shape[1] // 2
        theirs_at = pl.ds(pl.multiple_of((1 - core) * half + first, 128), width)
        _, where = cols(chunk)
        return remote(outs[array].at[:, :, :, :, where], outs[array].at[:, :, :, :, theirs_at], gs_send.at[chunk], gs_recv.at[chunk], sibling)

    floats = tok_ref[0].astype(f32)
    normed[...] = (rms_scaled(floats) * again_ref[...]).astype(bf16)
    loads = [local(src.at[0], dst, w_sem.at[i]) for i, (src, dst) in enumerate(((wg_hbm, wg), (wu_hbm, wu), (wd_hbm, wd)))]

    def matrix(ref, tile):
        return ref[:, :, :, :, tile * TILE:(tile + 1) * TILE].reshape(-1, TILE)

    ctx = (x // 2) * 2 + core
    peers = [device((x + 2) % NX, y, z, core), sibling, device((x + 2) % NX, y, z, 1 - core)]

    def make_keys():
        pair = jnp.dot(normed[...], matrix(kv_all, 0), preferred_element_type=f32)
        key_values[ctx, :, :HD] = rms_scaled(pair[:, :HD]).astype(bf16)
        key_values[ctx, :, HD:] = pair[:, HD:].astype(bf16)
        for peer in peers:
            remote(key_values.at[ctx], key_values.at[ctx], kv_send, kv_recv, peer).start()

    def kv_wait():
        three = key_values.at[pl.ds(0, 3)]
        return remote(three, three, kv_send, kv_recv, sibling)

    def make_queries(tile):
        wide = jnp.dot(normed[...], matrix(q_all, tile), preferred_element_type=f32)
        for head in range(TILE // HD):
            queries[tile * 2 + head] = rms_scaled(wide[:, head * HD:(head + 1) * HD]).astype(bf16)

    def attend(tile):
        keys = key_values[:, :, :HD].reshape(-1, HD)
        values = key_values[:, :, HD:].reshape(-1, HD)
        for head in (tile * 2, tile * 2 + 1):
            scores = lax.dot_general(queries[head], keys, (((1,), (1,)), ((), ())), preferred_element_type=f32) * (HD ** (-0.5))
            weights = jnp.exp(scores).astype(bf16)
            weighted = jnp.dot(weights, values, preferred_element_type=f32)
            totals = jnp.sum(weights.astype(f32), axis=1, keepdims=True)
            context[:, head * HD:(head + 1) * HD] = (weighted / totals).astype(bf16)

    def project(tile):
        att_ref[0, :, tile * TILE:(tile + 1) * TILE] = jnp.dot(context[...], matrix(o_all, tile), preferred_element_type=f32).astype(bf16)

    y_step(0)
    y_step(1)
    x_step(0)
    y_step(2)
    x_step(1)
    gs_step(0)
    gs_wait(0).wait_recv()
    make_keys()
    y_step(3)
    x_step(2)
    gs_step(1)
    gs_wait(1).wait_recv()
    make_queries(0)
    make_queries(2)
    y_step(4)
    x_step(3)
    lane = lax.broadcasted_iota(jnp.int32, (tokens, experts), 1)
    down, across = (lax.broadcasted_iota(jnp.int32, (tokens, tokens), i) for i in (0, 1))
    ids = [jnp.sum(jnp.where(across == down, id_ref[0, choice:choice + 1, :].astype(f32), 0.0), axis=1, keepdims=True).astype(jnp.int32) for choice in range(TOP)]
    named = [ids[choice] == lane for choice in range(TOP)]
    either = jnp.where(named[0] | named[1], 1.0, 0.0).astype(bf16)
    before = jnp.dot(jnp.where(across < down, 1.0, 0.0).astype(bf16), either, preferred_element_type=f32)
    sent_at = []
    for choice in range(TOP):
        slot = jnp.sum(jnp.where(named[choice], before, 0.0), axis=1, keepdims=True).astype(jnp.int32)
        chip, low = ids[choice] % (NZ * NY), ids[choice] // (NZ * NY)
        place = (((chip % NY) * NZ + chip // NY) * 2 + low) * high + slot
        back_ref[:, choice:choice + 1] = place
        place = jnp.sum(jnp.where(across == down, place.astype(f32), 0.0), axis=0, keepdims=True).astype(jnp.int32)
        sent_at.append(jnp.concatenate([place + q * CAP for q in range(Q)], axis=1))
    row = lax.broadcasted_iota(jnp.int32, (2 * NZ * NY * high, Q * tokens), 0)
    chosen_ref[...] = jnp.where((row == sent_at[0]) | (row == sent_at[1]), 1.0, 0.0).astype(bf16)
    for ref, a, b in ((into, 0, 1), (outof, 1, 0)):
        to, at = (lax.broadcasted_iota(jnp.int32, (NZ * high, NZ * high), i) for i in (a, b))
        same = (to // block == (at % high) // CAP) & ((to % block) // CAP == at // high) & (to % CAP == at % CAP)
        ref[...] = jnp.where(same, 1.0, 0.0).astype(bf16)
    gs_step(2)
    gs_wait(2).wait_recv()
    make_queries(1)
    make_queries(3)
    kv_wait().wait_recv()
    attend(0)
    x_step(4)
    attend(1)
    gs_step(3)
    attend(2)
    attend(3)
    gs_step(4)
    for load in loads:
        load.start()
    gs_wait(3).wait_recv()
    project(0)
    project(2)
    gs_wait(4).wait_recv()
    project(1)
    project(3)
    mixed = floats + att_ref[0].astype(f32)
    moe_ref[...] = (rms_scaled(mixed) * mgain_ref[...]).astype(bf16)

    def half_at(part):
        return ((z // (NZ // 2) + 1 + part) % 2) * (NZ // 2)

    def half_of(part):
        return pl.ds(half_at(part), NZ // 2)

    for q in range(Q):
        quarters[q] = moe_ref[:, q * W:(q + 1) * W]
    for d in (0, 1, 3, 2):
        to_y = (y + d) % NY
        part = chosen_ref[pl.ds(pl.multiple_of(to_y * (2 * NZ * high), 2 * NZ * high), 2 * NZ * high), :]
        sent[to_y] = jnp.dot(part, quarters[...].reshape(Q * tokens, W), preferred_element_type=f32).astype(bf16).reshape(NZ, 2, high, W)
        for part in range(2):
            for k in (3, 1, 2, 0):
                to_z = half_at(part) + (z + k) % (NZ // 2)
                if (k, d, part) != (0, 0, 1):
                    remote(sent.at[to_y, to_z], came.at[d, z], zy_send, zy_recv.at[d, part], device(x, to_y, to_z, core)).start()
    own_block = local(sent.at[y, z], came.at[0, z], own_sem.at[0])
    own_block.start()
    logits = lax.dot_general(moe_ref[...], router_ref[...], (((1,), (1,)), ((), ())), preferred_element_type=f32)
    picked = [jnp.sum(jnp.where(named[choice], logits, 0.0), axis=1, keepdims=True) for choice in range(TOP)]
    first = jax.nn.sigmoid(picked[0] - picked[1])
    gate_ref[:, 0:1] = first
    gate_ref[:, 1:2] = 1.0 - first

    def spread(d, part):
        where, count = half_of(part), NZ // 2 - (1 if (d, part) == (0, 1) else 0)
        some = came.at[d, pl.ds(half_at(part), count)]
        remote(some, some, zy_send, zy_recv.at[d, part], sibling).wait_recv()
        if (d, part) == (0, 1):
            own_block.wait()
        for k, low in ((2, x_lo), (1, 1 - x_lo), (3, 1 - x_lo)):
            remote(came.at[d, where, low], rows.at[d, core, k - 1, where], x_send.at[d], x_recv.at[d, part], device((x + k) % NX, y, z, core)).start()
        if part == 1:
            local(came.at[d, :, x_lo], rows.at[d, core, 3], own_sem.at[1 + d]).start()
            remote(came.at[d, :, x_lo], rows.at[d, core, 3], s_send.at[d], s_recv.at[d], sibling).start()

    def x_wait(d):
        three = rows.at[d, core, pl.ds(0, 3)]
        return remote(three, three, x_send.at[d], x_recv.at[d, 0], sibling)

    def share(d, part):
        three = rows.at[d, core, pl.ds(0, 3), half_of(part)]
        remote(three, three, x_send.at[d], x_recv.at[d, part], sibling).wait_recv()
        remote(three, three, s_send.at[d], s_recv.at[d], sibling).start()

    def s_wait(d):
        return remote(rows.at[d, core], rows.at[d, 1 - core], s_send.at[d], s_recv.at[d], sibling)

    def compute(d):
        s_wait(d).wait_recv()
        local(came.at[d, :, x_lo], rows.at[d, core, 3], own_sem.at[1 + d]).wait()
        if d == 0:
            for load in loads:
                load.wait()
        for group in range(2 * NX):
            turned = jnp.dot(into[...], rows[d, group // NX, group % NX].reshape(NZ * high, W), preferred_element_type=f32).astype(bf16)
            for q in range(Q):
                many[group * block:(group + 1) * block, q * W:(q + 1) * W] = turned[q * block:(q + 1) * block]

        gated = jnp.dot(many[...], wg[...], preferred_element_type=f32)
        lifted = jnp.dot(many[...], wu[...], preferred_element_type=f32)
        hidden[...] = (gated / (1.0 + jnp.exp(-gated)) * lifted).astype(bf16)
        outcome[...] = jnp.dot(hidden[...], wd[...], preferred_element_type=f32).astype(bf16)
        for group in range(2 * NX):
            flat = jnp.concatenate([outcome[group * block:(group + 1) * block, q * W:(q + 1) * W] for q in range(Q)], axis=0)
            turned = jnp.dot(outof[...], flat, preferred_element_type=f32).astype(bf16)
            terms[d, group // NX, group % NX] = turned.reshape(NZ, high, W)
        remote(terms.at[d, 1 - core], theirs.at[d], rs_send.at[d], rs_recv.at[d], sibling).start()

    def rs_wait(d):
        return remote(terms.at[d, 1 - core], theirs.at[d], rs_send.at[d], rs_recv.at[d], sibling)

    def halve(d):
        rs_wait(d).wait_recv()
        halves[d] = (terms[d, core].astype(f32) + theirs[d].astype(f32)).astype(bf16)
        for part in range(2):
            where = half_of(part)
            for k in (2, 1, 3):
                remote(halves.at[d, k - 1, where], sides.at[d, k - 1, where], rx_send.at[d], rx_recv.at[d, part], device((x - k + NX) % NX, y, z, core)).start()

    def rx_wait(d):
        return remote(halves.at[d, pl.ds(0, 3)], sides.at[d], rx_send.at[d], rx_recv.at[d, 0], sibling)

    def finish(d):
        for part in range(2):
            where = half_of(part)
            three = sides.at[d, :, where]
            remote(three, three, rx_send.at[d], rx_recv.at[d, part], sibling).wait_recv()
            final[d, where, x_lo] = (halves[d, 3, where].astype(f32) + sides[d, 1, where].astype(f32)).astype(bf16)
            final[d, where, 1 - x_lo] = (sides[d, 0, where].astype(f32) + sides[d, 2, where].astype(f32)).astype(bf16)
            for k in (3, 1, 2, 0):
                to_z, to_y = half_at(part) + (z + k) % (NZ // 2), (y - d + NY) % NY
                if (k, d, part) == (0, 0, 1):
                    local(final.at[d, z], back.at[y, z], own_sem.at[1 + NY]).start()
                else:
                    remote(final.at[d, to_z], back.at[y, z], rz_send, rz_recv.at[d], device(x, to_y, to_z, core)).start()

    def pick(d, first_pick=False):
        count, from_y = NZ if d else NZ - 1, (y + d) % NY
        part = back.at[from_y, pl.ds(0, count)]
        remote(part, part, rz_send, rz_recv.at[d], sibling).wait_recv()
        if d == 0:
            local(final.at[d, z], back.at[y, z], own_sem.at[1 + NY]).wait()
        place = lax.broadcasted_iota(jnp.int32, (tokens, 2 * NZ * high), 1) + from_y * (2 * NZ * high)
        got = back[from_y].reshape(2 * NZ * high, W)
        for q in range(Q):
            total = None
            for choice in range(TOP):
                mine = jnp.where(place == back_ref[:, choice:choice + 1] + q * CAP, 1.0, 0.0).astype(bf16)
                part = gate_ref[:, choice:choice + 1] * jnp.dot(mine, got, preferred_element_type=f32)
                total = part if total is None else total + part
            if first_pick:
                mix[:, q * W:(q + 1) * W] = total
            else:
                mix[:, q * W:(q + 1) * W] += total

    spread(0, 0)
    spread(0, 1)
    share(0, 0)
    spread(1, 0)
    share(0, 1)
    spread(1, 1)
    compute(0)
    share(1, 0)
    spread(3, 0)
    share(1, 1)
    halve(0)
    spread(3, 1)
    compute(1)
    share(3, 0)
    spread(2, 0)
    share(3, 1)
    halve(1)
    spread(2, 1)
    finish(0)
    compute(3)
    share(2, 0)
    share(2, 1)
    halve(3)
    finish(1)
    compute(2)
    pick(0, True)
    halve(2)
    finish(3)
    pick(1)
    finish(2)
    pick(3)
    pick(2)
    mix_ref[0] = mix[...].astype(bf16)

    for d in range(NY):
        x_wait(d).wait_send()
        s_wait(d).wait_send()
        rs_wait(d).wait_send()
        rx_wait(d).wait_send()
    for sent_ref, sem in ((came, zy_send), (final, rz_send)):
        some = sent_ref.at[pl.ds(0, NY - 1)]
        remote(some, some, sem, rz_recv.at[0], sibling).wait_send()
        rest = sent_ref.at[0, pl.ds(0, NZ - 1)]
        remote(rest, rest, sem, rz_recv.at[0], sibling).wait_send()
    for chunk in range(len(CHUNKS)):
        z_wait(chunk).wait_send()
        y_wait(chunk).wait_send()
        gx_wait(chunk).wait_send()
        gs_wait(chunk).wait_send()
    kv_wait().wait_send()


def settle(a_ref, b_ref, a_out, b_out):
    a_out[...] = a_ref[...]
    b_out[...] = b_ref[...]


def body(
    tokens, expert_ids, attn_gain, w_query, w_kv, w_out, moe_gain, router, w_gate, w_up, w_down
):
    _, rows, features = tokens.shape
    width = w_gate.shape[2]
    heads = w_query.shape[1] // HD
    block = (NZ, Q * CAP, W)
    piece = (2, Q * CAP, W)
    dma, vmem = pltpu.SemaphoreType.DMA, pltpu.VMEM
    n = len(CHUNKS)
    any_spec, vmem_spec = pl.BlockSpec(memory_space=pl.ANY), pl.BlockSpec(memory_space=vmem)
    results = pl.pallas_call(
        layer_kernel,
        out_shape=[jax.ShapeDtypeStruct(tokens.shape, bf16)] * 2,
        in_specs=[vmem_spec] * 5 + [any_spec] * 6,
        out_specs=[vmem_spec] * 2,
        scratch_shapes=[vmem((2, NZ, NY) + w.shape, bf16) for w in (w_query, w_kv, w_out)]
        + [
            vmem((rows, features), bf16),
            vmem((heads, rows, HD), bf16),
            vmem((4, rows, 2 * HD), bf16),
            vmem((rows, heads * HD), bf16),
            vmem((rows, features), bf16),
            vmem((Q, rows, W), bf16),
            vmem((2 * NZ * NY * Q * CAP, Q * rows), bf16),
            vmem((rows, TOP), jnp.int32),
            vmem((rows, TOP), f32),
            vmem((NZ * Q * CAP, NZ * Q * CAP), bf16),
            vmem((NZ * Q * CAP, NZ * Q * CAP), bf16),
            vmem((2 * NX * NZ * CAP, features), bf16),
            vmem((2 * NX * NZ * CAP, features), bf16),
            vmem((rows, features), f32),
            vmem((features, width), bf16),
            vmem((features, width), bf16),
            vmem((width, features), bf16),
            vmem((NY, NZ) + piece, bf16),
            vmem((NY, NZ) + piece, bf16),
            vmem((NY, 2, NX) + block, bf16),
            vmem((2 * NX * NZ * CAP, width), bf16),
            vmem((NY, 2, NX) + block, bf16),
            vmem((NY, NX) + block, bf16),
            vmem((NY, NX) + block, bf16),
            vmem((NY, NX - 1) + block, bf16),
            vmem((NY, NZ) + piece, bf16),
            vmem((NY, NZ) + piece, bf16),
        ]
        + [dma((n,))] * 9
        + [dma, dma]
        + [
            dma((3,)), dma, dma((NY, 2)), dma((NY,)), dma((NY, 2)), dma((NY,)), dma((NY,)), dma((2 + NY,)),
            dma((NY,)), dma((NY,)), dma((NY,)), dma((NY, 2)), dma, dma((NY,)),
        ],
        compiler_params=pltpu.CompilerParams(collective_id=0, has_side_effects=True, vmem_limit_bytes=60 << 20),
        name="layer",
    )(tokens, expert_ids.swapaxes(1, 2), attn_gain.reshape(1, -1), moe_gain.reshape(1, -1), router.T, w_query, w_kv, w_out, w_gate, w_up, w_down)
    return tuple(pl.pallas_call(
        settle,
        out_shape=[jax.ShapeDtypeStruct(tokens.shape, bf16)] * 2,
        in_specs=[vmem_spec] * 2,
        out_specs=[vmem_spec] * 2,
        name="settle",
    )(*results))


def solution(mesh):
    in_specs = (
        P("exp", "ctx", None),
        P("exp", "ctx", None),
        P(),
        P("exp", None),
        P("exp", None),
        P("exp", None),
        P(),
        P(),
        P("exp", None, "ctx"),
        P("exp", None, "ctx"),
        P("exp", "ctx", None),
    )
    out_specs = (P("exp", "ctx", None), P("exp", "ctx", None))
    return jax.shard_map(body, mesh=mesh, in_specs=in_specs, out_specs=out_specs, check_vma=False)
```

```python
import functools

import jax
import jax.numpy as jnp
from jax import lax
from jax.experimental import pallas as pl
from jax.experimental.pallas import tpu as pltpu
from jax.sharding import PartitionSpec as P

HD = 128
TOP = 2
MESH = pl.DeviceIdType.MESH
NX, NY, NZ = 4, 4, 8


epsilon = 1e-06
bf16, f32 = jnp.bfloat16, jnp.float32


def rms_scaled(values):
    return values * lax.rsqrt(jnp.mean(values * values, axis=-1, keepdims=True) + epsilon)


def here():
    ctx, exp = lax.axis_index("ctx"), lax.axis_index("exp")
    core, y = ctx % 2, exp % NY
    z, x_lo = (exp // NY) % NZ, exp // (NY * NZ)
    return (ctx // 2) * 2 + x_lo, y, z, core


def device(x, y, z, core):
    return (x // 2) * 2 + core, ((x % 2) * NZ + z) * NY + y


def signal(sem, target):
    pl.semaphore_signal(sem, inc=1, device_id=target, device_id_type=MESH)


CHUNKS = ((1, 0, 128), (0, 0, 256), (0, 256, 256), (2, 0, 256), (2, 256, 256))
TILE = 256
CAP = 6
Q, W = 4, 256


def remote(src, dst, send, recv, target):
    return pltpu.make_async_remote_copy(src_ref=src, dst_ref=dst, send_sem=send, recv_sem=recv, device_id=target, device_id_type=MESH)


def local(src, dst, sem):
    return pltpu.make_async_copy(src, dst, sem)


def layer_kernel(tok_ref, id_ref, again_ref, mgain_ref, router_ref, q_in, kv_in, o_in, wg_hbm, wu_hbm, wd_hbm, att_ref, mix_ref,
                 q_all, kv_all, o_all, normed, queries, key_values, context, moe_ref, quarters, chosen_ref, back_ref, gate_ref, into, outof, many, outcome, mix,
                 wg, wu, wd, sent, came, rows, hidden, terms, theirs, halves, sides, final, back,
                 g_own, z_send, z_recv, y_send, y_recv, gx_send, gx_recv, gs_send, gs_recv, kv_send, kv_recv,
                 w_sem, zy_send, zy_recv, x_send, x_recv, s_send, s_recv, own_sem,
                 rs_send, rs_recv, rx_send, rx_recv, rz_send, rz_recv):
    x, y, z, core = here()
    x_lo = x % 2
    features = tok_ref.shape[2]
    tokens = tok_ref.shape[1]
    experts = router_ref.shape[0]
    block = NZ * CAP
    high = Q * CAP
    sibling = device(x, y, z, 1 - core)
    barrier = pltpu.get_barrier_semaphore()
    partners = [device(x, y, (z + k) % NZ, core) for k in range(1, NZ)] + [device(x, (y + k) % NY, z, core) for k in range(1, NY)]
    partners += [device((x + k) % NX, y, z, core) for k in range(1, NX)]
    partners += [sibling, device((x + 2) % NX, y, z, 1 - core)]
    for partner in partners:
        signal(barrier, partner)

    ins, outs = (q_in, kv_in, o_in), (q_all, kv_all, o_all)

    def cols(chunk):
        array, first, width = CHUNKS[chunk]
        half = ins[array].shape[1] // 2
        return array, pl.ds(pl.multiple_of(core * half + first, 128), width)

    own = []
    for chunk in range(len(CHUNKS)):
        array, where = cols(chunk)
        copy = local(ins[array].at[:, where], outs[array].at[x_lo, z, y, :, where], g_own.at[chunk])
        copy.start()
        own.append(copy)
    pl.semaphore_wait(barrier, len(partners))
    for chunk in range(len(CHUNKS)):
        array, where = cols(chunk)
        for k in (4, 3, 5, 2, 6, 1, 7):
            remote(ins[array].at[:, where], outs[array].at[x_lo, z, y, :, where], z_send.at[chunk], z_recv.at[chunk],
                   device(x, y, (z + k) % NZ, core)).start()

    def z_wait(chunk):
        array, where = cols(chunk)
        seven = outs[array].at[x_lo, pl.ds(0, NZ - 1), y, :, where]
        return remote(seven, seven, z_send.at[chunk], z_recv.at[chunk], sibling)

    def y_step(chunk):
        array, where = cols(chunk)
        z_wait(chunk).wait_recv()
        own[chunk].wait()
        part = outs[array].at[x_lo, :, y, :, where]
        for k in (2, 1, 3):
            remote(part, part, y_send.at[chunk], y_recv.at[chunk], device(x, (y + k) % NY, z, core)).start()

    def y_wait(chunk):
        array, where = cols(chunk)
        three = outs[array].at[x_lo, :, pl.ds(0, NY - 1), :, where]
        return remote(three, three, y_send.at[chunk], y_recv.at[chunk], sibling)

    def x_step(chunk):
        array, where = cols(chunk)
        y_wait(chunk).wait_recv()
        for k, first in ((1, 0), (3, NZ // 2)):
            part = outs[array].at[x_lo, pl.ds(first, NZ // 2), :, :, where]
            remote(part, part, gx_send.at[chunk], gx_recv.at[chunk], device((x + k) % NX, y, z, core)).start()
        part = outs[array].at[x_lo, :, :, :, where]
        remote(part, part, gs_send.at[chunk], gs_recv.at[chunk], sibling).start()

    def gx_wait(chunk):
        array, where = cols(chunk)
        mine, other = outs[array].at[x_lo, :, :, :, where], outs[array].at[1 - x_lo, :, :, :, where]
        return remote(mine, other, gx_send.at[chunk], gx_recv.at[chunk], sibling)

    def gs_step(chunk):
        array, where = cols(chunk)
        gx_wait(chunk).wait_recv()
        part = outs[array].at[1 - x_lo, :, :, :, where]
        remote(part, part, gs_send.at[chunk], gs_recv.at[chunk], sibling).start()

    def gs_wait(chunk):
        array, first, width = CHUNKS[chunk]
        half = ins[array].shape[1] // 2
        theirs_at = pl.ds(pl.multiple_of((1 - core) * half + first, 128), width)
        _, where = cols(chunk)
        return remote(outs[array].at[:, :, :, :, where], outs[array].at[:, :, :, :, theirs_at], gs_send.at[chunk], gs_recv.at[chunk], sibling)

    floats = tok_ref[0].astype(f32)
    normed[...] = (rms_scaled(floats) * again_ref[...]).astype(bf16)
    loads = [local(src.at[0], dst, w_sem.at[i]) for i, (src, dst) in enumerate(((wg_hbm, wg), (wu_hbm, wu), (wd_hbm, wd)))]

    def matrix(ref, tile):
        return ref[:, :, :, :, tile * TILE:(tile + 1) * TILE].reshape(-1, TILE)

    ctx = (x // 2) * 2 + core
    peers = [device((x + 2) % NX, y, z, core), sibling, device((x + 2) % NX, y, z, 1 - core)]

    def make_keys():
        pair = jnp.dot(normed[...], matrix(kv_all, 0), preferred_element_type=f32)
        key_values[ctx, :, :HD] = rms_scaled(pair[:, :HD]).astype(bf16)
        key_values[ctx, :, HD:] = pair[:, HD:].astype(bf16)
        for peer in peers:
            remote(key_values.at[ctx], key_values.at[ctx], kv_send, kv_recv, peer).start()

    def kv_wait():
        three = key_values.at[pl.ds(0, 3)]
        return remote(three, three, kv_send, kv_recv, sibling)

    def make_queries(tile):
        wide = jnp.dot(normed[...], matrix(q_all, tile), preferred_element_type=f32)
        for head in range(TILE // HD):
            queries[tile * 2 + head] = rms_scaled(wide[:, head * HD:(head + 1) * HD]).astype(bf16)

    def attend(tile):
        keys = key_values[:, :, :HD].reshape(-1, HD)
        values = key_values[:, :, HD:].reshape(-1, HD)
        for head in (tile * 2, tile * 2 + 1):
            scores = lax.dot_general(queries[head], keys, (((1,), (1,)), ((), ())), preferred_element_type=f32) * (HD ** (-0.5))
            weights = jnp.exp(scores).astype(bf16)
            weighted = jnp.dot(weights, values, preferred_element_type=f32)
            totals = jnp.sum(weights.astype(f32), axis=1, keepdims=True)
            context[:, head * HD:(head + 1) * HD] = (weighted / totals).astype(bf16)

    def project(tile):
        att_ref[0, :, tile * TILE:(tile + 1) * TILE] = jnp.dot(context[...], matrix(o_all, tile), preferred_element_type=f32).astype(bf16)

    y_step(0)
    y_step(1)
    x_step(0)
    y_step(2)
    x_step(1)
    gs_step(0)
    gs_wait(0).wait_recv()
    make_keys()
    y_step(3)
    x_step(2)
    gs_step(1)
    gs_wait(1).wait_recv()
    make_queries(0)
    make_queries(2)
    y_step(4)
    x_step(3)
    lane = lax.broadcasted_iota(jnp.int32, (tokens, experts), 1)
    down, across = (lax.broadcasted_iota(jnp.int32, (tokens, tokens), i) for i in (0, 1))
    ids = [jnp.sum(jnp.where(across == down, id_ref[0, choice:choice + 1, :].astype(f32), 0.0), axis=1, keepdims=True).astype(jnp.int32) for choice in range(TOP)]
    named = [ids[choice] == lane for choice in range(TOP)]
    either = jnp.where(named[0] | named[1], 1.0, 0.0).astype(bf16)
    before = jnp.dot(jnp.where(across < down, 1.0, 0.0).astype(bf16), either, preferred_element_type=f32)
    sent_at = []
    for choice in range(TOP):
        slot = jnp.sum(jnp.where(named[choice], before, 0.0), axis=1, keepdims=True).astype(jnp.int32)
        chip, low = ids[choice] % (NZ * NY), ids[choice] // (NZ * NY)
        place = (((chip % NY) * NZ + chip // NY) * 2 + low) * high + slot
        back_ref[:, choice:choice + 1] = place
        place = jnp.sum(jnp.where(across == down, place.astype(f32), 0.0), axis=0, keepdims=True).astype(jnp.int32)
        sent_at.append(jnp.concatenate([place + q * CAP for q in range(Q)], axis=1))
    row = lax.broadcasted_iota(jnp.int32, (2 * NZ * NY * high, Q * tokens), 0)
    chosen_ref[...] = jnp.where((row == sent_at[0]) | (row == sent_at[1]), 1.0, 0.0).astype(bf16)
    for ref, a, b in ((into, 0, 1), (outof, 1, 0)):
        to, at = (lax.broadcasted_iota(jnp.int32, (NZ * high, NZ * high), i) for i in (a, b))
        same = (to // block == (at % high) // CAP) & ((to % block) // CAP == at // high) & (to % CAP == at % CAP)
        ref[...] = jnp.where(same, 1.0, 0.0).astype(bf16)
    gs_step(2)
    gs_wait(2).wait_recv()
    make_queries(1)
    make_queries(3)
    x_step(4)
    kv_wait().wait_recv()
    attend(0)
    attend(1)
    gs_step(3)
    attend(2)
    attend(3)
    gs_step(4)
    for load in loads:
        load.start()
    gs_wait(3).wait_recv()
    project(0)
    project(2)
    gs_wait(4).wait_recv()
    project(1)
    project(3)
    mixed = floats + att_ref[0].astype(f32)
    moe_ref[...] = (rms_scaled(mixed) * mgain_ref[...]).astype(bf16)

    def half_at(part):
        return ((z // (NZ // 2) + 1 + part) % 2) * (NZ // 2)

    def half_of(part):
        return pl.ds(half_at(part), NZ // 2)

    for q in range(Q):
        quarters[q] = moe_ref[:, q * W:(q + 1) * W]
    for d in (1, 2, 3, 0):
        to_y = (y + d) % NY
        part = chosen_ref[pl.ds(pl.multiple_of(to_y * (2 * NZ * high), 2 * NZ * high), 2 * NZ * high), :]
        sent[to_y] = jnp.dot(part, quarters[...].reshape(Q * tokens, W), preferred_element_type=f32).astype(bf16).reshape(NZ, 2, high, W)
        for part in range(2):
            for k in (3, 1, 2, 0):
                to_z = half_at(part) + (z + k) % (NZ // 2)
                if (k, d, part) != (0, 0, 1):
                    remote(sent.at[to_y, to_z], came.at[d, z], zy_send, zy_recv.at[d, part], device(x, to_y, to_z, core)).start()
    own_block = local(sent.at[y, z], came.at[0, z], own_sem.at[0])
    own_block.start()
    logits = lax.dot_general(moe_ref[...], router_ref[...], (((1,), (1,)), ((), ())), preferred_element_type=f32)
    picked = [jnp.sum(jnp.where(named[choice], logits, 0.0), axis=1, keepdims=True) for choice in range(TOP)]
    first = jax.nn.sigmoid(picked[0] - picked[1])
    gate_ref[:, 0:1] = first
    gate_ref[:, 1:2] = 1.0 - first

    def spread(d, part):
        where, count = half_of(part), NZ // 2 - (1 if (d, part) == (0, 1) else 0)
        some = came.at[d, pl.ds(half_at(part), count)]
        remote(some, some, zy_send, zy_recv.at[d, part], sibling).wait_recv()
        if (d, part) == (0, 1):
            own_block.wait()
        for k, low in ((2, x_lo), (1, 1 - x_lo), (3, 1 - x_lo)):
            remote(came.at[d, where, low], rows.at[d, core, k - 1, where], x_send.at[d], x_recv.at[d, part], device((x + k) % NX, y, z, core)).start()
        if part == 1:
            local(came.at[d, :, x_lo], rows.at[d, core, 3], own_sem.at[1 + d]).start()
            remote(came.at[d, :, x_lo], rows.at[d, core, 3], s_send.at[d], s_recv.at[d], sibling).start()

    def x_wait(d):
        three = rows.at[d, core, pl.ds(0, 3)]
        return remote(three, three, x_send.at[d], x_recv.at[d, 0], sibling)

    def share(d, part):
        three = rows.at[d, core, pl.ds(0, 3), half_of(part)]
        remote(three, three, x_send.at[d], x_recv.at[d, part], sibling).wait_recv()
        remote(three, three, s_send.at[d], s_recv.at[d], sibling).start()

    def s_wait(d):
        return remote(rows.at[d, core], rows.at[d, 1 - core], s_send.at[d], s_recv.at[d], sibling)

    def compute(d):
        s_wait(d).wait_recv()
        local(came.at[d, :, x_lo], rows.at[d, core, 3], own_sem.at[1 + d]).wait()
        if d == 1:
            for load in loads:
                load.wait()
        for group in range(2 * NX):
            turned = jnp.dot(into[...], rows[d, group // NX, group % NX].reshape(NZ * high, W), preferred_element_type=f32).astype(bf16)
            for q in range(Q):
                many[group * block:(group + 1) * block, q * W:(q + 1) * W] = turned[q * block:(q + 1) * block]

        gated = jnp.dot(many[...], wg[...], preferred_element_type=f32)
        lifted = jnp.dot(many[...], wu[...], preferred_element_type=f32)
        hidden[...] = (gated / (1.0 + jnp.exp(-gated)) * lifted).astype(bf16)
        outcome[...] = jnp.dot(hidden[...], wd[...], preferred_element_type=f32).astype(bf16)
        for group in range(2 * NX):
            flat = jnp.concatenate([outcome[group * block:(group + 1) * block, q * W:(q + 1) * W] for q in range(Q)], axis=0)
            turned = jnp.dot(outof[...], flat, preferred_element_type=f32).astype(bf16)
            terms[d, group // NX, group % NX] = turned.reshape(NZ, high, W)
        remote(terms.at[d, 1 - core], theirs.at[d], rs_send.at[d], rs_recv.at[d], sibling).start()

    def rs_wait(d):
        return remote(terms.at[d, 1 - core], theirs.at[d], rs_send.at[d], rs_recv.at[d], sibling)

    def halve(d):
        rs_wait(d).wait_recv()
        halves[d] = (terms[d, core].astype(f32) + theirs[d].astype(f32)).astype(bf16)
        for part in range(2):
            where = half_of(part)
            for k in (2, 1, 3):
                remote(halves.at[d, k - 1, where], sides.at[d, k - 1, where], rx_send.at[d], rx_recv.at[d, part], device((x - k + NX) % NX, y, z, core)).start()

    def rx_wait(d):
        return remote(halves.at[d, pl.ds(0, 3)], sides.at[d], rx_send.at[d], rx_recv.at[d, 0], sibling)

    def finish(d):
        for part in range(2):
            where = half_of(part)
            three = sides.at[d, :, where]
            remote(three, three, rx_send.at[d], rx_recv.at[d, part], sibling).wait_recv()
            final[d, where, x_lo] = (halves[d, 3, where].astype(f32) + sides[d, 1, where].astype(f32)).astype(bf16)
            final[d, where, 1 - x_lo] = (sides[d, 0, where].astype(f32) + sides[d, 2, where].astype(f32)).astype(bf16)
            for k in (3, 1, 2, 0):
                to_z, to_y = half_at(part) + (z + k) % (NZ // 2), (y - d + NY) % NY
                if (k, d, part) == (0, 0, 1):
                    local(final.at[d, z], back.at[y, z], own_sem.at[1 + NY]).start()
                else:
                    remote(final.at[d, to_z], back.at[y, z], rz_send, rz_recv.at[d], device(x, to_y, to_z, core)).start()

    def pick(d, first_pick=False):
        count, from_y = NZ if d else NZ - 1, (y + d) % NY
        part = back.at[from_y, pl.ds(0, count)]
        remote(part, part, rz_send, rz_recv.at[d], sibling).wait_recv()
        if d == 0:
            local(final.at[d, z], back.at[y, z], own_sem.at[1 + NY]).wait()
        place = lax.broadcasted_iota(jnp.int32, (tokens, 2 * NZ * high), 1) + from_y * (2 * NZ * high)
        got = back[from_y].reshape(2 * NZ * high, W)
        for q in range(Q):
            total = None
            for choice in range(TOP):
                mine = jnp.where(place == back_ref[:, choice:choice + 1] + q * CAP, 1.0, 0.0).astype(bf16)
                part = gate_ref[:, choice:choice + 1] * jnp.dot(mine, got, preferred_element_type=f32)
                total = part if total is None else total + part
            if first_pick:
                mix[:, q * W:(q + 1) * W] = total
            else:
                mix[:, q * W:(q + 1) * W] += total

    spread(1, 0)
    spread(1, 1)
    share(1, 0)
    spread(2, 0)
    share(1, 1)
    spread(2, 1)
    compute(1)
    share(2, 0)
    spread(3, 0)
    share(2, 1)
    halve(1)
    spread(3, 1)
    compute(2)
    share(3, 0)
    spread(0, 0)
    share(3, 1)
    halve(2)
    spread(0, 1)
    finish(1)
    compute(3)
    share(0, 0)
    share(0, 1)
    halve(3)
    finish(2)
    compute(0)
    pick(1, True)
    halve(0)
    finish(3)
    pick(2)
    finish(0)
    pick(3)
    pick(0)
    mix_ref[0] = mix[...].astype(bf16)

    for d in range(NY):
        x_wait(d).wait_send()
        s_wait(d).wait_send()
        rs_wait(d).wait_send()
        rx_wait(d).wait_send()
    for sent_ref, sem in ((came, zy_send), (final, rz_send)):
        some = sent_ref.at[pl.ds(0, NY - 1)]
        remote(some, some, sem, rz_recv.at[0], sibling).wait_send()
        rest = sent_ref.at[0, pl.ds(0, NZ - 1)]
        remote(rest, rest, sem, rz_recv.at[0], sibling).wait_send()
    for chunk in range(len(CHUNKS)):
        z_wait(chunk).wait_send()
        y_wait(chunk).wait_send()
        gx_wait(chunk).wait_send()
        gs_wait(chunk).wait_send()
    kv_wait().wait_send()


def settle(a_ref, b_ref, a_out, b_out):
    a_out[...] = a_ref[...]
    b_out[...] = b_ref[...]


def body(
    tokens, expert_ids, attn_gain, w_query, w_kv, w_out, moe_gain, router, w_gate, w_up, w_down
):
    _, rows, features = tokens.shape
    width = w_gate.shape[2]
    heads = w_query.shape[1] // HD
    block = (NZ, Q * CAP, W)
    piece = (2, Q * CAP, W)
    dma, vmem = pltpu.SemaphoreType.DMA, pltpu.VMEM
    n = len(CHUNKS)
    any_spec, vmem_spec = pl.BlockSpec(memory_space=pl.ANY), pl.BlockSpec(memory_space=vmem)
    results = pl.pallas_call(
        layer_kernel,
        out_shape=[jax.ShapeDtypeStruct(tokens.shape, bf16)] * 2,
        in_specs=[vmem_spec] * 5 + [any_spec] * 6,
        out_specs=[vmem_spec] * 2,
        scratch_shapes=[vmem((2, NZ, NY) + w.shape, bf16) for w in (w_query, w_kv, w_out)]
        + [
            vmem((rows, features), bf16),
            vmem((heads, rows, HD), bf16),
            vmem((4, rows, 2 * HD), bf16),
            vmem((rows, heads * HD), bf16),
            vmem((rows, features), bf16),
            vmem((Q, rows, W), bf16),
            vmem((2 * NZ * NY * Q * CAP, Q * rows), bf16),
            vmem((rows, TOP), jnp.int32),
            vmem((rows, TOP), f32),
            vmem((NZ * Q * CAP, NZ * Q * CAP), bf16),
            vmem((NZ * Q * CAP, NZ * Q * CAP), bf16),
            vmem((2 * NX * NZ * CAP, features), bf16),
            vmem((2 * NX * NZ * CAP, features), bf16),
            vmem((rows, features), f32),
            vmem((features, width), bf16),
            vmem((features, width), bf16),
            vmem((width, features), bf16),
            vmem((NY, NZ) + piece, bf16),
            vmem((NY, NZ) + piece, bf16),
            vmem((NY, 2, NX) + block, bf16),
            vmem((2 * NX * NZ * CAP, width), bf16),
            vmem((NY, 2, NX) + block, bf16),
            vmem((NY, NX) + block, bf16),
            vmem((NY, NX) + block, bf16),
            vmem((NY, NX - 1) + block, bf16),
            vmem((NY, NZ) + piece, bf16),
            vmem((NY, NZ) + piece, bf16),
        ]
        + [dma((n,))] * 9
        + [dma, dma]
        + [
            dma((3,)), dma, dma((NY, 2)), dma((NY,)), dma((NY, 2)), dma((NY,)), dma((NY,)), dma((2 + NY,)),
            dma((NY,)), dma((NY,)), dma((NY,)), dma((NY, 2)), dma, dma((NY,)),
        ],
        compiler_params=pltpu.CompilerParams(collective_id=0, has_side_effects=True, vmem_limit_bytes=60 << 20),
        name="layer",
    )(tokens, expert_ids.swapaxes(1, 2), attn_gain.reshape(1, -1), moe_gain.reshape(1, -1), router.T, w_query, w_kv, w_out, w_gate, w_up, w_down)
    return tuple(pl.pallas_call(
        settle,
        out_shape=[jax.ShapeDtypeStruct(tokens.shape, bf16)] * 2,
        in_specs=[vmem_spec] * 2,
        out_specs=[vmem_spec] * 2,
        name="settle",
    )(*results))


def solution(mesh):
    in_specs = (
        P("exp", "ctx", None),
        P("exp", "ctx", None),
        P(),
        P("exp", None),
        P("exp", None),
        P("exp", None),
        P(),
        P(),
        P("exp", None, "ctx"),
        P("exp", None, "ctx"),
        P("exp", "ctx", None),
    )
    out_specs = (P("exp", "ctx", None), P("exp", "ctx", None))
    return jax.shard_map(body, mesh=mesh, in_specs=in_specs, out_specs=out_specs, check_vma=False)
```
